32 devices in a mesh: groups: 2 (over x), tm: 8 (over z, y), space: 2 (over core).
Axes of the slice: x: 2, y: 2, z: 4, core: 2. Of those that a mesh axis runs over, the one named last changes fastest.
Arguments:
- query: bfloat16 [32, 16, 16, 1024], P(('groups', 'tm'), 'space'), parts along dimension 0, may hold values from -50 to 50
- key_in: bfloat16 [32, 16, 16, 1024], P(('groups', 'tm'), 'space'), parts along dimension 0, may hold values from -7 to 7
- value: bfloat16 [32, 16, 16, 1024], P(('groups', 'tm'), 'space'), parts along dimension 0, may hold values from -6 to 6
- upstream: bfloat16 [32, 16, 16, 1024], P(('groups', 'tm'), 'space'), parts along dimension 0, may hold values from -6 to 6
- conv_weight: float32 [3, 1024], replicated, may hold values from -3 to 3
- block_mask: int32 [8, 8], replicated, may hold values from 0 to 1, as said below
Outputs:
- output: bfloat16 [32, 16, 16, 1024], P(('groups', 'tm'), 'space'), parts along dimension 0
- grad_query: bfloat16 [32, 16, 16, 1024], P(('groups', 'tm'), 'space'), parts along dimension 0
- grad_key: bfloat16 [32, 16, 16, 1024], P(('groups', 'tm'), 'space'), parts along dimension 0
- grad_value: bfloat16 [32, 16, 16, 1024], P(('groups', 'tm'), 'space'), parts along dimension 0
The draws below stay inside these ranges and needn't reach their ends.
There are 2 independent parts, one for each index of `groups`. The reference program is written for one: setup_inputs(seed, part) draws one part's arguments, and reference() takes and returns one part's arrays. A program takes and returns all parts, laid end to end along the dimension named above; an argument that names none is the same for every part. Nothing has to cross between parts.
Inputs may be any that keep to these rules, and one draw needn't show every extreme that they name: block_mask[i][i] is 1; block_mask[i][j] is 0 where j > i or i - j >= 2; in between either value.
All inputs are finite; a program needn't handle non-finite values.
Results may differ from the reference program's by a relative error of at most 0.0072.
Values may be sent and summed in bfloat16 or wider, within the bound.
A program may use at most 128 MiB of HBM per device.

```python
import jax
import jax.numpy as jnp
from jax import lax

HEADS = 8
HD = 128
FB = 2
NY = 16
DA = 1024
NX = 16
NF = 16
WIN = 2
N_TM = 8


def query_key_pair(key):
    shape = (NF, NX, NY, HEADS * HD)
    keys = jnp.clip(jax.random.normal(jax.random.fold_in(key, 11), shape, jnp.float32), -6.0, 6.0)
    queries = jnp.clip(2.5 * jax.random.normal(jax.random.fold_in(key, 12), shape, jnp.float32), -15.0, 15.0)
    return (queries, keys)


def draw_query(key, part):
    return query_key_pair(key)[0].astype(jnp.bfloat16)


def draw_key_in(key, part):
    return query_key_pair(key)[1].astype(jnp.bfloat16)


def draw_block_mask(key, part):
    rows = jax.lax.broadcasted_iota(jnp.int32, (N_TM, N_TM), 0)
    cols = jax.lax.broadcasted_iota(jnp.int32, (N_TM, N_TM), 1)
    lag = rows - cols
    coin = jax.random.randint(jax.random.fold_in(key, 21), (N_TM, N_TM), 0, 4)
    inside = jnp.logical_and(jnp.logical_and(lag > 0, lag < WIN), coin != 0)
    keep = jnp.logical_or(lag == 0, inside)
    return keep.astype(jnp.int32)


def level_of(rng, extent, shards, low, high):
    factor_of = 1.0
    for dim, parts in shards:
        draws = jax.random.uniform(jax.random.fold_in(jax.random.fold_in(rng, 6), dim), (parts,), jnp.float32, low / len(shards), high / len(shards))
        factor_of = factor_of * jnp.repeat(jnp.exp(draws), extent[dim] // parts).reshape((-1,) + (1,) * (len(extent) - 1 - dim))
    return factor_of


def scatter_about(stream_key, dims, spread, limit, split=(), held_as=jnp.bfloat16):
    array = spread * jax.random.normal(stream_key, dims, jnp.float32)
    if split:
        array = array * level_of(stream_key, dims, split, -0.22, 0.18)
    return jnp.clip(array, -limit, limit).astype(held_as)


def setup_inputs(seed: int = 0, part: int = 0) -> dict:
    key_list = jax.random.split(jax.random.key(seed), 7)
    own_keys = jax.random.split(jax.random.fold_in(key_list[6], part), 7)
    return {
        "query": draw_query(jax.random.fold_in(jax.random.fold_in(key_list[6], part), 71), part),
        "key_in": draw_key_in(jax.random.fold_in(jax.random.fold_in(key_list[6], part), 71), part),
        "value": scatter_about(own_keys[2], (NF, NX, NY, DA), 1.0, 6.0, ((0, 8), (1, 2))),
        "upstream": scatter_about(own_keys[3], (NF, NX, NY, DA), 1.0, 6.0, ((0, 8), (1, 2))),
        "conv_weight": scatter_about(key_list[4], (3, DA), 0.5, 3.0, (), jnp.float32),
        "block_mask": draw_block_mask(jax.random.fold_in(key_list[6], 71), part),
    }


def reference(query, key_in, value, upstream, conv_weight, block_mask):
    width = HEADS * HD
    block_rows = FB * NX * NY
    nblocks = N_TM
    win = WIN
    scale = 1.0 / (HD ** 0.5)
    qb = query.reshape(nblocks, block_rows, HEADS, HD)
    kb = key_in.reshape(nblocks, block_rows, HEADS, HD)
    vb = value.reshape(nblocks, block_rows, HEADS, HD)
    db = upstream.reshape(nblocks, block_rows, HEADS, HD)
    zero_pad = jnp.zeros((win - 1, block_rows, HEADS, HD), jnp.bfloat16)
    keys_pad = jnp.concatenate([zero_pad, kb], axis=0)
    vals_pad = jnp.concatenate([zero_pad, vb], axis=0)
    mask_pad = jnp.concatenate([jnp.zeros((nblocks, win - 1), jnp.int32), block_mask.astype(jnp.int32)], axis=1)

    def step(carry, blk):
        grad_kp, grad_vp = carry
        qh = lax.dynamic_index_in_dim(qb, blk, 0, False).astype(jnp.float32)
        dh = lax.dynamic_index_in_dim(db, blk, 0, False).astype(jnp.float32)
        kh = lax.dynamic_slice_in_dim(keys_pad, blk, win, 0).reshape(win * block_rows, HEADS, HD).astype(jnp.float32)
        vh = lax.dynamic_slice_in_dim(vals_pad, blk, win, 0).reshape(win * block_rows, HEADS, HD).astype(jnp.float32)
        mrow = lax.dynamic_index_in_dim(mask_pad, blk, 0, False)
        window = lax.dynamic_slice_in_dim(mrow, blk, win, 0)
        keep = jnp.repeat(window, block_rows, total_repeat_length=win * block_rows) > 0
        scores = jnp.einsum('rhd,khd->hrk', qh, kh) * scale
        scores = jnp.where(keep[None, None, :], scores, -jnp.inf)
        top = jnp.max(scores, axis=-1, keepdims=True)
        expo = jnp.exp(scores - top)
        probs = expo / jnp.sum(expo, axis=-1, keepdims=True)
        probs_low = probs.astype(jnp.bfloat16).astype(jnp.float32)
        attended = jnp.einsum('hrk,khd->rhd', probs_low, vh)
        dprobs = jnp.einsum('rhd,khd->hrk', dh, vh)
        delta = jnp.sum(dh * attended, axis=-1)
        dscores = (probs * (dprobs - jnp.transpose(delta)[:, :, None]) * scale).astype(jnp.bfloat16).astype(jnp.float32)
        grad_q = jnp.einsum('hrk,khd->rhd', dscores, kh)
        grad_k = jnp.einsum('hrk,rhd->khd', dscores, qh).reshape(win, block_rows, HEADS, HD)
        grad_v = jnp.einsum('hrk,rhd->khd', probs_low, dh).reshape(win, block_rows, HEADS, HD)
        grad_kp = lax.dynamic_update_slice_in_dim(grad_kp, lax.dynamic_slice_in_dim(grad_kp, blk, win, 0) + grad_k, blk, 0)
        grad_vp = lax.dynamic_update_slice_in_dim(grad_vp, lax.dynamic_slice_in_dim(grad_vp, blk, win, 0) + grad_v, blk, 0)
        return (grad_kp, grad_vp), (attended, grad_q)

    start = jnp.zeros((nblocks + win - 1, block_rows, HEADS, HD), jnp.float32)
    (grad_kp, grad_vp), (attended, grad_q) = lax.scan(step, (start, start), jnp.arange(nblocks, dtype=jnp.int32))
    shape = (NF, NX, NY, width)
    attended = attended.reshape(shape)
    grad_q = grad_q.reshape(shape)
    grad_k = grad_kp[win - 1:].reshape(shape)
    grad_v = grad_vp[win - 1:].reshape(shape)
    vals = value.astype(jnp.float32)
    ups = upstream.astype(jnp.float32)
    w = conv_weight
    lepe = w[0] * jnp.roll(vals, 1, axis=1) + w[1] * vals + w[2] * jnp.roll(vals, -1, axis=1)
    conv_back = w[0] * jnp.roll(ups, -1, axis=1) + w[1] * ups + w[2] * jnp.roll(ups, 1, axis=1)
    output = (attended + lepe).astype(jnp.bfloat16)
    return output, grad_q.astype(jnp.bfloat16), grad_k.astype(jnp.bfloat16), (grad_v + conv_back).astype(jnp.bfloat16)
```

```python
import functools
import math

import jax
import jax.numpy as jnp
from jax import lax
from jax.experimental import pallas as pl
from jax.experimental.pallas import tpu as pltpu
from jax.sharding import PartitionSpec as P

HD = 128
MESH = pl.DeviceIdType.MESH
F32 = jnp.float32
BF16 = jnp.bfloat16
NT = (((1,), (1,)), ((), ()))


def kernel(
    n, ns, win, frames, radial,
    q_ref, k_ref, v_ref, d_ref, w_ref, mask_ref,
    o_ref, gq_ref, gk_ref, gv_ref,
    pair, kv, st, ob, gb, gr, ac, ar, rf, rb,
    lx, sx_s, sx_r, f_s, f_r, g_s, g_r, ob_s, ob_r, ac_s, ac_r,
    rf_s, rf_r, rb_s, rb_r,
):
    i = lax.axis_index("tm")
    s = lax.axis_index("space")
    rows, width = q_ref.shape
    heads = width // HD // ns
    block = ns * rows
    lags = win - 1
    scale = 1.0 / math.sqrt(HD)
    ins = (q_ref, k_ref, v_ref, d_ref)
    relay = win == 2 and n % 2 == 0
    planes = max(1, n // 2)
    plane = i // 2
    odd = lax.rem(i, 2) == 1
    via_ahead = heads * (planes - 1 - plane) // planes
    via_back = heads * plane // planes

    def cols(slot, h):
        return pl.ds(pl.multiple_of((slot * heads + h) * HD, HD), HD)

    def slab(slot):
        return pl.ds(pl.multiple_of(slot * rows, rows), rows)

    def peer(shift):
        return lax.rem(s + shift, ns)

    def source(shift):
        return lax.rem(s + ns - shift, ns)

    def own_copy(a, h):
        return pltpu.make_async_copy(
            ins[a].at[:, cols(s, h)], pair.at[a, h, slab(s)], lx.at[a, h]
        )

    def pair_copy(shift, a, h):
        return pltpu.make_async_remote_copy(
            src_ref=ins[a].at[:, cols(peer(shift), h)],
            dst_ref=pair.at[a, h, slab(s)],
            send_sem=sx_s.at[shift - 1, a, h],
            recv_sem=sx_r.at[shift - 1, a, h],
            device_id={"space": peer(shift)},
            device_id_type=MESH,
        )

    def ahead_copy(lag, a, h, slot, sem_slot):
        return pltpu.make_async_remote_copy(
            src_ref=ins[1 + a].at[:, cols(slot, h)],
            dst_ref=kv.at[lag - 1, a, h, slab(s)],
            send_sem=f_s.at[lag - 1, a, h, slot],
            recv_sem=f_r.at[lag - 1, a, h, sem_slot],
            device_id={"tm": i + lag, "space": slot},
            device_id_type=MESH,
        )

    def back_copy(lag, a, h, slot, sem_slot):
        return pltpu.make_async_remote_copy(
            src_ref=gb.at[lag - 1, a, h, pl.ds(slot * rows, rows)],
            dst_ref=gr.at[lag - 1, a, h, s],
            send_sem=g_s.at[lag - 1, a, h, slot],
            recv_sem=g_r.at[lag - 1, a, h, sem_slot],
            device_id={"tm": i - lag, "space": slot},
            device_id_type=MESH,
        )

    def ahead_first(a, h, slot, sem_slot):
        return pltpu.make_async_remote_copy(
            src_ref=ins[1 + a].at[:, cols(slot, h)],
            dst_ref=rf.at[a, h, slab(s)],
            send_sem=f_s.at[0, a, h, slot],
            recv_sem=rf_r.at[a, h, sem_slot],
            device_id={"tm": i - 1, "space": slot},
            device_id_type=MESH,
        )

    def ahead_second(a, h, src):
        return pltpu.make_async_remote_copy(
            src_ref=rf.at[a, h, slab(src)],
            dst_ref=kv.at[0, a, h, slab(src)],
            send_sem=rf_s.at[a, h, src],
            recv_sem=f_r.at[0, a, h, src],
            device_id={"tm": i + 2},
            device_id_type=MESH,
        )

    def back_first(a, h, slot, sem_slot):
        return pltpu.make_async_remote_copy(
            src_ref=gb.at[0, a, h, pl.ds(slot * rows, rows)],
            dst_ref=rb.at[a, h, s],
            send_sem=g_s.at[0, a, h, slot],
            recv_sem=rb_r.at[a, h, sem_slot],
            device_id={"tm": i + 1, "space": slot},
            device_id_type=MESH,
        )

    def back_second(a, h, src):
        return pltpu.make_async_remote_copy(
            src_ref=rb.at[a, h, src],
            dst_ref=gr.at[0, a, h, src],
            send_sem=rb_s.at[a, h, src],
            recv_sem=g_r.at[0, a, h, src],
            device_id={"tm": i - 2},
            device_id_type=MESH,
        )

    def out_copy(shift, b, h):
        return pltpu.make_async_remote_copy(
            src_ref=ob.at[b, h, slab(peer(shift))],
            dst_ref=(o_ref, gq_ref)[b].at[:, cols(s, h)],
            send_sem=ob_s.at[shift - 1, b, h],
            recv_sem=ob_r.at[shift - 1, b, h],
            device_id={"space": peer(shift)},
            device_id_type=MESH,
        )

    def own_grad_copy(shift, a, h):
        return pltpu.make_async_remote_copy(
            src_ref=ac.at[a, h, slab(peer(shift))],
            dst_ref=ar.at[shift - 1, a, h],
            send_sem=ac_s.at[shift - 1, a, h],
            recv_sem=ac_r.at[shift - 1, a, h],
            device_id={"space": peer(shift)},
            device_id_type=MESH,
        )

    barrier = pltpu.get_barrier_semaphore()
    count = ns - 1
    for shift in range(1, ns):
        pl.semaphore_signal(barrier, inc=1, device_id={"space": peer(shift)}, device_id_type=MESH)
    for lag in range(1, win):
        for there, here in ((i + lag, i + lag < n), (i - lag, i >= lag)):
            count = count + ns * jnp.where(here, 1, 0)

            @pl.when(here)
            def _():
                for slot in range(ns):
                    pl.semaphore_signal(
                        barrier, inc=1, device_id={"tm": there, "space": slot}, device_id_type=MESH
                    )
    pl.semaphore_wait(barrier, count)


    def direct(here, far):
        return here if far is None else jnp.logical_and(here, jnp.logical_not(far))

    def send_inputs(h, carry):
        for lag in range(1, win):
            far = jnp.logical_and(odd, h >= heads - via_ahead) if relay else None

            @pl.when(direct(i + lag < n, far))
            def _():
                for a in range(2):
                    for slot in range(ns):
                        ahead_copy(lag, a, h, slot, s).start()

        if relay:

            @pl.when(jnp.logical_and(i + 1 < n, far))
            def _():
                for a in range(2):
                    for slot in range(ns):
                        ahead_first(a, h, slot, s).start()

        for a in range(4):
            for shift in range(1, ns):
                pair_copy(shift, a, h).start()
            own_copy(a, h).start()
        return carry

    lax.fori_loop(0, heads, send_inputs, 0)

    for lag in range(1, win):

        @pl.when(i < lag)
        def _():
            kv[lag - 1] = jnp.zeros(kv.shape[1:], BF16)

    biases = [None]
    for lag in range(1, win):
        allowed = jnp.logical_and(i >= lag, mask_ref[i, jnp.maximum(i - lag, 0)] > 0)
        biases.append(jnp.where(allowed, 0.0, -jnp.inf).astype(F32))

    part = rows
    chunks = [(lag, c) for lag in range(win) for c in range(block // part)]
    span = rows // frames

    def neighbours(a, h):
        low, high = [], []
        for slot in range(ns):
            before, after = (slot + ns - 1) % ns * rows, (slot + 1) % ns * rows
            for f in range(frames):
                at = f * span
                here = slot * rows + at
                low.append(pair[a, h, before + at + span - radial : before + at + span, :])
                low.append(pair[a, h, here : here + span - radial, :])
                high.append(pair[a, h, here + radial : here + span, :])
                high.append(pair[a, h, after + at : after + at + radial, :])
        return (
            jnp.concatenate(low, axis=0).astype(F32),
            jnp.concatenate(high, axis=0).astype(F32),
        )

    def send_terms(h, carry):
        far = jnp.logical_and(jnp.logical_not(odd), h < via_back) if relay else None
        for lag in range(1, win):

            @pl.when(direct(i >= lag, far))
            def _():
                for a in range(2):
                    for slot in range(ns):
                        back_copy(lag, a, h, slot, s).start()

        if relay:

            @pl.when(jnp.logical_and(i >= 1, far))
            def _():
                for a in range(2):
                    for slot in range(ns):
                        back_first(a, h, slot, s).start()

        return carry

    def head(h, carry):
        if relay:

            @pl.when(jnp.logical_and(jnp.logical_and(jnp.logical_not(odd), i + 2 < n), h < via_ahead))
            def _():
                late = heads - via_ahead + h
                for a in range(2):
                    for src in range(ns):
                        ahead_first(a, late, src, src).wait_recv()
                        ahead_second(a, late, src).start()

        for a in range(4):
            own_copy(a, h).wait()
            for shift in range(1, ns):
                pair_copy(shift, a, h).wait_recv()
        for lag in range(1, win):

            @pl.when(i >= lag)
            def _():
                for a in range(2):
                    for slot in range(ns):
                        ahead_copy(lag, a, h, slot, slot).wait_recv()

        sent_now = jnp.where(odd, 0, via_back) if relay else 0
        if relay:
            first = jnp.where(odd, heads // 2, heads - 1)
            sent = jnp.where(odd, 0, jnp.minimum(via_back, heads - 1))
        else:
            first, sent = heads - 1, 0

        @pl.when(h == first)
        def _():
            lax.fori_loop(sent, first, send_terms, 0)

        q = pair[0, h]
        d = pair[3, h]

        def keys(lag, c):
            at = slice(c * part, (c + 1) * part)
            return pair[1, h, at, :] if lag == 0 else kv[lag - 1, 0, h, at, :]

        def vals(lag, c):
            at = slice(c * part, (c + 1) * part)
            return pair[2, h, at, :] if lag == 0 else kv[lag - 1, 1, h, at, :]

        top = None
        for j, (lag, c) in enumerate(chunks):
            sc = lax.dot_general(keys(lag, c), q, NT, preferred_element_type=F32)
            if lag:
                sc = sc + biases[lag]
            st[j * part : (j + 1) * part, :] = sc
            high = jnp.max(sc, axis=0, keepdims=True)
            top = high if top is None else jnp.maximum(top, high)
        total = None
        att = None
        factor = scale * math.log2(math.e)
        for j, (lag, c) in enumerate(chunks):
            p = jnp.exp2((st[j * part : (j + 1) * part, :] - top) * factor)
            st[j * part : (j + 1) * part, :] = p
            add = jnp.sum(p, axis=0, keepdims=True)
            total = add if total is None else total + add
            term = jnp.dot(vals(lag, c).T, p.astype(BF16), preferred_element_type=F32)
            att = term if att is None else att + term
        inv = 1.0 / total
        att = att * inv
        delta = jnp.sum(d.T.astype(F32) * att, axis=0, keepdims=True)
        v_low, v_high = neighbours(2, h)
        d_low, d_high = neighbours(3, h)
        w0 = w_ref[0:1, cols(s, h)]
        w1 = w_ref[1:2, cols(s, h)]
        w2 = w_ref[2:3, cols(s, h)]
        lepe = w0 * v_low + w1 * pair[2, h].astype(F32) + w2 * v_high
        conv_back = w0 * d_high + w1 * d.astype(F32) + w2 * d_low
        ob[0, h] = (att.T + lepe).astype(BF16)
        gq = None
        for j, (lag, c) in reversed(list(enumerate(chunks))):
            at = slice(c * part, (c + 1) * part)
            dp = lax.dot_general(vals(lag, c), d, NT, preferred_element_type=F32)
            p = st[j * part : (j + 1) * part, :] * inv
            gv = jnp.dot(p.astype(BF16), d, preferred_element_type=F32)
            ds = (p * (dp - delta)).astype(BF16)
            gk = jnp.dot(ds, q, preferred_element_type=F32) * scale
            term = jnp.dot(keys(lag, c).T, ds, preferred_element_type=F32)
            gq = term if gq is None else gq + term
            if lag:
                gb[lag - 1, 0, h, at, :] = gk.astype(BF16)
                gb[lag - 1, 1, h, at, :] = gv.astype(BF16)
            else:
                ac[0, h, at, :] = gk
                ac[1, h, at, :] = gv + conv_back[at]
        ob[1, h] = (gq * scale).T.astype(BF16)

        @pl.when(jnp.logical_or(h >= first, h < sent_now))
        def _():
            send_terms(h, 0)

        for shift in range(1, ns):
            for b in range(2):
                out_copy(shift, b, h).start()
                own_grad_copy(shift, b, h).start()
        o_ref[:, cols(s, h)] = ob[0, h, slab(s), :]
        gq_ref[:, cols(s, h)] = ob[1, h, slab(s), :]
        return carry

    lax.fori_loop(0, heads, head, 0)

    def drain(h, carry):
        for shift in range(1, ns):
            for a in range(4):
                pair_copy(shift, a, h).wait_send()
            for b in range(2):
                out_copy(shift, b, h).wait()
                own_grad_copy(shift, b, h).wait_send()
        for lag in range(1, win):
            for a in range(2):
                for slot in range(ns):

                    @pl.when(i + lag < n)
                    def _():
                        ahead_copy(lag, a, h, slot, s).wait_send()

        return carry

    def relay_back(h, carry):
        @pl.when(jnp.logical_and(jnp.logical_and(odd, i >= 2), h < via_back))
        def _():
            for a in range(2):
                for src in range(ns):
                    back_first(a, h, src, src).wait_recv()
                    back_second(a, h, src).start()

        return carry

    if relay:
        lax.fori_loop(0, heads, relay_back, 0)
    lax.fori_loop(0, heads, drain, 0)

    def finish(h, carry):
        for shift in range(ns):
            slot = source(shift)
            for a in range(2):
                if shift:
                    own_grad_copy(shift, a, h).wait_recv()
                    base = ar.at[shift - 1, a, h]
                else:
                    base = ac.at[a, h, slab(s)]
                for lag in range(1, win):

                    @pl.when(i + lag < n)
                    def _():
                        pltpu.make_async_remote_copy(
                            src_ref=gb.at[lag - 1, a, h, slab(slot)],
                            dst_ref=gr.at[lag - 1, a, h, slot],
                            send_sem=g_s.at[lag - 1, a, h, slot],
                            recv_sem=g_r.at[lag - 1, a, h, slot],
                            device_id={"space": peer(1)},
                            device_id_type=MESH,
                        ).wait_recv()
                        base[...] = base[...] + gr[lag - 1, a, h, slot].astype(F32)

                (gk_ref, gv_ref)[a][:, cols(slot, h)] = base[...].astype(BF16)
        return carry

    lax.fori_loop(0, heads, finish, 0)

    def drain_back(h, carry):
        for lag in range(1, win):

            @pl.when(i >= lag)
            def _():
                for a in range(2):
                    for slot in range(ns):
                        back_copy(lag, a, h, slot, s).wait_send()

        return carry

    lax.fori_loop(0, heads, drain_back, 0)

    def drain_relays(h, carry):
        @pl.when(jnp.logical_and(jnp.logical_and(jnp.logical_not(odd), i + 2 < n), h >= heads - via_ahead))
        def _():
            for a in range(2):
                for src in range(ns):
                    ahead_second(a, h, src).wait_send()

        @pl.when(jnp.logical_and(jnp.logical_and(odd, i >= 2), h < via_back))
        def _():
            for a in range(2):
                for src in range(ns):
                    back_second(a, h, src).wait_send()

        return carry

    if relay:
        lax.fori_loop(0, heads, drain_relays, 0)


def hand_on(*refs):
    sems = refs[-1]
    half = len(refs) // 2
    copies = [pltpu.make_async_copy(refs[j], refs[half + j], sems.at[j]) for j in range(half)]
    for copy in copies:
        copy.start()
    for copy in copies:
        copy.wait()


def local(query, key_in, value, upstream, conv_weight, block_mask):
    frames, cells, radial, width = query.shape
    n = lax.axis_size("tm")
    ns = lax.axis_size("space")
    win = max(2, n // 8)
    lags = win - 1
    rows = frames * cells * radial
    heads = width // HD // ns
    block = ns * rows
    flat = [x.reshape(rows, width) for x in (query, key_in, value, upstream)]
    dma = pltpu.SemaphoreType.DMA
    vmem = pl.BlockSpec(memory_space=pltpu.VMEM)
    outs = pl.pallas_call(
        functools.partial(kernel, n, ns, win, frames, radial),
        out_shape=[pltpu.VMEM((rows, width), BF16)] * 4,
        in_specs=[pl.BlockSpec(memory_space=pltpu.HBM)] * 4 + [vmem] + [pl.BlockSpec(memory_space=pltpu.SMEM)],
        out_specs=[vmem] * 4,
        scratch_shapes=[
            pltpu.VMEM((4, heads, block, HD), BF16),
            pltpu.VMEM((lags, 2, heads, block, HD), BF16),
            pltpu.VMEM((win * block, block), F32),
            pltpu.VMEM((2, heads, block, HD), BF16),
            pltpu.VMEM((lags, 2, heads, block, HD), BF16),
            pltpu.VMEM((lags, 2, heads, ns, rows, HD), BF16),
            pltpu.VMEM((2, heads, block, HD), F32),
            pltpu.VMEM((ns - 1, 2, heads, rows, HD), F32),
            pltpu.VMEM((2, heads, block, HD), BF16),
            pltpu.VMEM((2, heads, ns, rows, HD), BF16),
            dma((4, heads)),
            dma((ns - 1, 4, heads)),
            dma((ns - 1, 4, heads)),
            dma((lags, 2, heads, ns)),
            dma((lags, 2, heads, ns)),
            dma((lags, 2, heads, ns)),
            dma((lags, 2, heads, ns)),
            dma((ns - 1, 2, heads)),
            dma((ns - 1, 2, heads)),
            dma((ns - 1, 2, heads)),
            dma((ns - 1, 2, heads)),
            dma((2, heads, ns)),
            dma((2, heads, ns)),
            dma((2, heads, ns)),
            dma((2, heads, ns)),
        ],
        compiler_params=pltpu.CompilerParams(
            collective_id=0, has_side_effects=True, vmem_limit_bytes=123 * 2**19
        ),
    )(*flat, conv_weight, block_mask)
    outs = pl.pallas_call(
        hand_on,
        out_shape=[jax.ShapeDtypeStruct((rows, width), BF16)] * 4,
        in_specs=[vmem] * 4,
        out_specs=[pl.BlockSpec(memory_space=pl.ANY)] * 4,
        scratch_shapes=[dma((4,))],
        compiler_params=pltpu.CompilerParams(vmem_limit_bytes=8 * 2**20),
    )(*outs)
    return tuple(x.reshape(query.shape) for x in outs)


def solution(mesh):
    spec = P(("groups", "tm"), "space", None, None)
    return jax.shard_map(
        local,
        mesh=mesh,
        in_specs=(spec, spec, spec, spec, P(), P()),
        out_specs=(spec, spec, spec, spec),
        check_vma=False,
    )
```

```python
import functools
import math

import jax
import jax.numpy as jnp
from jax import lax
from jax.experimental import pallas as pl
from jax.experimental.pallas import tpu as pltpu
from jax.sharding import PartitionSpec as P

HD = 128
MESH = pl.DeviceIdType.MESH
F32 = jnp.float32
BF16 = jnp.bfloat16
NT = (((1,), (1,)), ((), ()))


def kernel(
    n, ns, win, frames, radial,
    q_ref, k_ref, v_ref, d_ref, w_ref, mask_ref,
    o_ref, gq_ref, gk_ref, gv_ref,
    pair, kv, st, ob, gb, gr, ac, ar, rf, rb,
    lx, sx_s, sx_r, f_s, f_r, g_s, g_r, ob_s, ob_r, ac_s, ac_r,
    rf_s, rf_r, rb_s, rb_r,
):
    i = lax.axis_index("tm")
    s = lax.axis_index("space")
    rows, width = q_ref.shape
    heads = width // HD // ns
    block = ns * rows
    lags = win - 1
    scale = 1.0 / math.sqrt(HD)
    ins = (q_ref, k_ref, v_ref, d_ref)
    relay = win == 2 and n % 2 == 0
    planes = max(1, n // 2)
    plane = i // 2
    odd = lax.rem(i, 2) == 1
    even = jnp.logical_not(odd)
    via_ahead = heads * (planes - 1 - plane) // planes
    share = max(0, 2 * heads * ns // planes - 1)
    via_back = share * plane
    gate = (share * (plane - 1) + 2 * ns - 1) // (2 * ns) - 1

    def cols(slot, h):
        return pl.ds(pl.multiple_of((slot * heads + h) * HD, HD), HD)

    def slab(slot):
        return pl.ds(pl.multiple_of(slot * rows, rows), rows)

    def peer(shift):
        return lax.rem(s + shift, ns)

    def source(shift):
        return lax.rem(s + ns - shift, ns)

    def own_copy(a, h):
        return pltpu.make_async_copy(
            ins[a].at[:, cols(s, h)], pair.at[a, h, slab(s)], lx.at[a, h]
        )

    def pair_copy(shift, a, h):
        return pltpu.make_async_remote_copy(
            src_ref=ins[a].at[:, cols(peer(shift), h)],
            dst_ref=pair.at[a, h, slab(s)],
            send_sem=sx_s.at[shift - 1, a, h],
            recv_sem=sx_r.at[shift - 1, a, h],
            device_id={"space": peer(shift)},
            device_id_type=MESH,
        )

    def ahead_copy(lag, a, h, slot, sem_slot):
        return pltpu.make_async_remote_copy(
            src_ref=ins[1 + a].at[:, cols(slot, h)],
            dst_ref=kv.at[lag - 1, a, h, slab(s)],
            send_sem=f_s.at[lag - 1, a, h, slot],
            recv_sem=f_r.at[lag - 1, a, h, sem_slot],
            device_id={"tm": i + lag, "space": slot},
            device_id_type=MESH,
        )

    def back_copy(lag, a, h, slot, sem_slot):
        return pltpu.make_async_remote_copy(
            src_ref=gb.at[lag - 1, a, h, pl.ds(slot * rows, rows)],
            dst_ref=gr.at[lag - 1, a, h, s],
            send_sem=g_s.at[lag - 1, a, h, slot],
            recv_sem=g_r.at[lag - 1, a, h, sem_slot],
            device_id={"tm": i - lag, "space": slot},
            device_id_type=MESH,
        )

    def ahead_first(a, h, slot, sem_slot):
        return pltpu.make_async_remote_copy(
            src_ref=ins[1 + a].at[:, cols(slot, h)],
            dst_ref=rf.at[a, h, slab(s)],
            send_sem=f_s.at[0, a, h, slot],
            recv_sem=rf_r.at[a, h, sem_slot],
            device_id={"tm": i - 1, "space": slot},
            device_id_type=MESH,
        )

    def ahead_second(a, h, src):
        return pltpu.make_async_remote_copy(
            src_ref=rf.at[a, h, slab(src)],
            dst_ref=kv.at[0, a, h, slab(src)],
            send_sem=rf_s.at[a, h, src],
            recv_sem=f_r.at[0, a, h, src],
            device_id={"tm": i + 2},
            device_id_type=MESH,
        )

    def back_first(a, h, slot, sem_slot):
        return pltpu.make_async_remote_copy(
            src_ref=gb.at[0, a, h, pl.ds(slot * rows, rows)],
            dst_ref=rb.at[a, h, s],
            send_sem=g_s.at[0, a, h, slot],
            recv_sem=rb_r.at[a, h, sem_slot],
            device_id={"tm": i + 1, "space": slot},
            device_id_type=MESH,
        )

    def back_second(a, h, src):
        return pltpu.make_async_remote_copy(
            src_ref=rb.at[a, h, src],
            dst_ref=gr.at[0, a, h, src],
            send_sem=rb_s.at[a, h, src],
            recv_sem=g_r.at[0, a, h, src],
            device_id={"tm": i - 2},
            device_id_type=MESH,
        )

    def out_copy(shift, b, h):
        return pltpu.make_async_remote_copy(
            src_ref=ob.at[b, h, slab(peer(shift))],
            dst_ref=(o_ref, gq_ref)[b].at[:, cols(s, h)],
            send_sem=ob_s.at[shift - 1, b, h],
            recv_sem=ob_r.at[shift - 1, b, h],
            device_id={"space": peer(shift)},
            device_id_type=MESH,
        )

    def own_grad_copy(shift, a, h):
        return pltpu.make_async_remote_copy(
            src_ref=ac.at[a, h, slab(peer(shift))],
            dst_ref=ar.at[shift - 1, a, h],
            send_sem=ac_s.at[shift - 1, a, h],
            recv_sem=ac_r.at[shift - 1, a, h],
            device_id={"space": peer(shift)},
            device_id_type=MESH,
        )

    barrier = pltpu.get_barrier_semaphore()
    count = ns - 1
    for shift in range(1, ns):
        pl.semaphore_signal(barrier, inc=1, device_id={"space": peer(shift)}, device_id_type=MESH)
    for lag in range(1, win):
        for there, here in ((i + lag, i + lag < n), (i - lag, i >= lag)):
            count = count + ns * jnp.where(here, 1, 0)

            @pl.when(here)
            def _():
                for slot in range(ns):
                    pl.semaphore_signal(
                        barrier, inc=1, device_id={"tm": there, "space": slot}, device_id_type=MESH
                    )
    pl.semaphore_wait(barrier, count)


    def direct(here, far):
        return here if far is None else jnp.logical_and(here, jnp.logical_not(far))

    def send_inputs(h, carry):
        for lag in range(1, win):
            far = jnp.logical_and(odd, h >= heads - via_ahead) if relay else None

            @pl.when(direct(i + lag < n, far))
            def _():
                for a in range(2):
                    for slot in range(ns):
                        ahead_copy(lag, a, h, slot, s).start()

        if relay:

            @pl.when(jnp.logical_and(i + 1 < n, far))
            def _():
                for a in range(2):
                    for slot in range(ns):
                        ahead_first(a, h, slot, s).start()

        for a in range(4):
            for shift in range(1, ns):
                pair_copy(shift, a, h).start()
            own_copy(a, h).start()
        return carry

    lax.fori_loop(0, heads, send_inputs, 0)

    for lag in range(1, win):

        @pl.when(i < lag)
        def _():
            kv[lag - 1] = jnp.zeros(kv.shape[1:], BF16)

    biases = [None]
    for lag in range(1, win):
        allowed = jnp.logical_and(i >= lag, mask_ref[i, jnp.maximum(i - lag, 0)] > 0)
        biases.append(jnp.where(allowed, 0.0, -jnp.inf).astype(F32))

    chunks = [(lag, c) for lag in range(win) for c in range(ns)]
    span = rows // frames

    def neighbours(a, h):
        low, high = [], []
        for slot in range(ns):
            before, after = (slot + ns - 1) % ns * rows, (slot + 1) % ns * rows
            for f in range(frames):
                at = f * span
                here = slot * rows + at
                low.append(pair[a, h, before + at + span - radial : before + at + span, :])
                low.append(pair[a, h, here : here + span - radial, :])
                high.append(pair[a, h, here + radial : here + span, :])
                high.append(pair[a, h, after + at : after + at + radial, :])
        return (
            jnp.concatenate(low, axis=0).astype(F32),
            jnp.concatenate(high, axis=0).astype(F32),
        )

    def part(a, h, slot):
        return (2 * h + a) * ns + slot

    def send_relayed(h, carry):
        for a in range(2):
            for slot in range(ns):

                @pl.when(jnp.logical_and(jnp.logical_and(even, i >= 1), part(a, h, slot) < via_back))
                def _():
                    back_first(a, h, slot, s).start()

        return carry

    def send_terms(h, carry):
        for lag in range(1, win):
            for a in range(2):
                for slot in range(ns):
                    near = jnp.logical_or(odd, part(a, h, slot) >= via_back) if relay else None

                    @pl.when(i >= lag if near is None else jnp.logical_and(i >= lag, near))
                    def _():
                        back_copy(lag, a, h, slot, s).start()

        return carry

    def head(h, carry):
        if relay:

            @pl.when(jnp.logical_and(jnp.logical_and(jnp.logical_not(odd), i + 2 < n), h < via_ahead))
            def _():
                late = heads - via_ahead + h
                for a in range(2):
                    for src in range(ns):
                        ahead_first(a, late, src, src).wait_recv()
                        ahead_second(a, late, src).start()

        for a in range(4):
            own_copy(a, h).wait()
            for shift in range(1, ns):
                pair_copy(shift, a, h).wait_recv()
        for lag in range(1, win):

            @pl.when(i >= lag)
            def _():
                for a in range(2):
                    for slot in range(ns):
                        ahead_copy(lag, a, h, slot, slot).wait_recv()

        if relay:
            first = jnp.where(odd, heads // 2, jnp.where(gate < 1, heads - 1, heads))
            middle = jnp.logical_and(even, gate < 0)
        else:
            first = heads - 1

        start = h == first
        if relay:
            start = jnp.logical_and(start, jnp.logical_not(middle))

        @pl.when(start)
        def _():
            lax.fori_loop(0, first, send_terms, 0)

        q = pair[0, h]
        d = pair[3, h]

        def keys(lag, c):
            at = slice(c * rows, (c + 1) * rows)
            return pair[1, h, at, :] if lag == 0 else kv[lag - 1, 0, h, at, :]

        def vals(lag, c):
            at = slice(c * rows, (c + 1) * rows)
            return pair[2, h, at, :] if lag == 0 else kv[lag - 1, 1, h, at, :]

        top = None
        for j, (lag, c) in enumerate(chunks):
            sc = lax.dot_general(keys(lag, c), q, NT, preferred_element_type=F32)
            if lag:
                sc = sc + biases[lag]
            st[j * rows : (j + 1) * rows, :] = sc
            high = jnp.max(sc, axis=0, keepdims=True)
            top = high if top is None else jnp.maximum(top, high)
        total = None
        att = None
        factor = scale * math.log2(math.e)
        for j, (lag, c) in enumerate(chunks):
            p = jnp.exp2((st[j * rows : (j + 1) * rows, :] - top) * factor)
            st[j * rows : (j + 1) * rows, :] = p
            add = jnp.sum(p, axis=0, keepdims=True)
            total = add if total is None else total + add
            term = jnp.dot(vals(lag, c).T, p.astype(BF16), preferred_element_type=F32)
            att = term if att is None else att + term
        inv = 1.0 / total
        att = att * inv
        delta = jnp.sum(d.T.astype(F32) * att, axis=0, keepdims=True)
        v_low, v_high = neighbours(2, h)
        d_low, d_high = neighbours(3, h)
        w0 = w_ref[0:1, cols(s, h)]
        w1 = w_ref[1:2, cols(s, h)]
        w2 = w_ref[2:3, cols(s, h)]
        lepe = w0 * v_low + w1 * pair[2, h].astype(F32) + w2 * v_high
        conv_back = w0 * d_high + w1 * d.astype(F32) + w2 * d_low
        ob[0, h] = (att.T + lepe).astype(BF16)
        if relay:

            @pl.when(jnp.logical_and(middle, h == max(0, heads - 2)))
            def _():
                lax.fori_loop(0, max(0, heads - 2), send_terms, 0)

        gq = None
        for j, (lag, c) in reversed(list(enumerate(chunks))):
            at = slice(c * rows, (c + 1) * rows)
            dp = lax.dot_general(vals(lag, c), d, NT, preferred_element_type=F32)
            p = st[j * rows : (j + 1) * rows, :] * inv
            gv = jnp.dot(p.astype(BF16), d, preferred_element_type=F32)
            ds = (p * (dp - delta)).astype(BF16)
            gk = jnp.dot(ds, q, preferred_element_type=F32) * scale
            term = jnp.dot(keys(lag, c).T, ds, preferred_element_type=F32)
            gq = term if gq is None else gq + term
            if lag:
                gb[lag - 1, 0, h, at, :] = gk.astype(BF16)
                gb[lag - 1, 1, h, at, :] = gv.astype(BF16)
            else:
                ac[0, h, at, :] = gk
                ac[1, h, at, :] = gv + conv_back[at]
        ob[1, h] = (gq * scale).T.astype(BF16)

        if relay:
            send_relayed(h, 0)

        now = h >= first
        if relay:
            now = jnp.logical_or(now, jnp.logical_and(middle, h >= heads - 2))

        @pl.when(now)
        def _():
            send_terms(h, 0)

        for shift in range(1, ns):
            for b in range(2):
                out_copy(shift, b, h).start()
                own_grad_copy(shift, b, h).start()
        o_ref[:, cols(s, h)] = ob[0, h, slab(s), :]
        gq_ref[:, cols(s, h)] = ob[1, h, slab(s), :]
        return carry

    lax.fori_loop(0, heads, head, 0)

    def drain(h, carry):
        for shift in range(1, ns):
            for a in range(4):
                pair_copy(shift, a, h).wait_send()
            for b in range(2):
                out_copy(shift, b, h).wait()
                own_grad_copy(shift, b, h).wait_send()
        for lag in range(1, win):
            for a in range(2):
                for slot in range(ns):

                    @pl.when(i + lag < n)
                    def _():
                        ahead_copy(lag, a, h, slot, s).wait_send()

        return carry

    def relay_back(h, carry):
        for a in range(2):

            @pl.when(jnp.logical_and(jnp.logical_and(odd, i >= 2), part(a, h, s) < via_back))
            def _():
                for src in range(ns):
                    back_first(a, h, src, src).wait_recv()
                    back_second(a, h, src).start()

        return carry

    if relay:
        lax.fori_loop(0, heads, relay_back, 0)
    lax.fori_loop(0, heads, drain, 0)

    def finish(h, carry):
        for shift in range(ns):
            slot = source(shift)
            for a in range(2):
                if shift:
                    own_grad_copy(shift, a, h).wait_recv()
                    base = ar.at[shift - 1, a, h]
                else:
                    base = ac.at[a, h, slab(s)]
                for lag in range(1, win):

                    @pl.when(i + lag < n)
                    def _():
                        pltpu.make_async_remote_copy(
                            src_ref=gb.at[lag - 1, a, h, slab(slot)],
                            dst_ref=gr.at[lag - 1, a, h, slot],
                            send_sem=g_s.at[lag - 1, a, h, slot],
                            recv_sem=g_r.at[lag - 1, a, h, slot],
                            device_id={"space": peer(1)},
                            device_id_type=MESH,
                        ).wait_recv()
                        base[...] = base[...] + gr[lag - 1, a, h, slot].astype(F32)

                (gk_ref, gv_ref)[a][:, cols(slot, h)] = base[...].astype(BF16)
            if relay and shift == 0:

                @pl.when(jnp.logical_and(jnp.logical_and(even, gate >= 1), h == gate))
                def _():
                    lax.fori_loop(0, heads, send_terms, 0)

        return carry

    lax.fori_loop(0, heads, finish, 0)

    def drain_back(h, carry):
        for lag in range(1, win):

            @pl.when(i >= lag)
            def _():
                for a in range(2):
                    for slot in range(ns):
                        back_copy(lag, a, h, slot, s).wait_send()

        return carry

    lax.fori_loop(0, heads, drain_back, 0)

    def drain_relays(h, carry):
        @pl.when(jnp.logical_and(jnp.logical_and(jnp.logical_not(odd), i + 2 < n), h >= heads - via_ahead))
        def _():
            for a in range(2):
                for src in range(ns):
                    ahead_second(a, h, src).wait_send()

        for a in range(2):

            @pl.when(jnp.logical_and(jnp.logical_and(odd, i >= 2), part(a, h, s) < via_back))
            def _():
                for src in range(ns):
                    back_second(a, h, src).wait_send()

        return carry

    if relay:
        lax.fori_loop(0, heads, drain_relays, 0)


def hand_on(*refs):
    sems = refs[-1]
    half = len(refs) // 2
    copies = [pltpu.make_async_copy(refs[j], refs[half + j], sems.at[j]) for j in range(half)]
    for copy in copies:
        copy.start()
    for copy in copies:
        copy.wait()


def local(query, key_in, value, upstream, conv_weight, block_mask):
    frames, cells, radial, width = query.shape
    n = lax.axis_size("tm")
    ns = lax.axis_size("space")
    win = max(2, n // 8)
    lags = win - 1
    rows = frames * cells * radial
    heads = width // HD // ns
    block = ns * rows
    flat = [x.reshape(rows, width) for x in (query, key_in, value, upstream)]
    dma = pltpu.SemaphoreType.DMA
    vmem = pl.BlockSpec(memory_space=pltpu.VMEM)
    outs = pl.pallas_call(
        functools.partial(kernel, n, ns, win, frames, radial),
        out_shape=[pltpu.VMEM((rows, width), BF16)] * 4,
        in_specs=[pl.BlockSpec(memory_space=pltpu.HBM)] * 4 + [vmem] + [pl.BlockSpec(memory_space=pltpu.SMEM)],
        out_specs=[vmem] * 4,
        scratch_shapes=[
            pltpu.VMEM((4, heads, block, HD), BF16),
            pltpu.VMEM((lags, 2, heads, block, HD), BF16),
            pltpu.VMEM((win * block, block), F32),
            pltpu.VMEM((2, heads, block, HD), BF16),
            pltpu.VMEM((lags, 2, heads, block, HD), BF16),
            pltpu.VMEM((lags, 2, heads, ns, rows, HD), BF16),
            pltpu.VMEM((2, heads, block, HD), F32),
            pltpu.VMEM((ns - 1, 2, heads, rows, HD), F32),
            pltpu.VMEM((2, heads, block, HD), BF16),
            pltpu.VMEM((2, heads, ns, rows, HD), BF16),
            dma((4, heads)),
            dma((ns - 1, 4, heads)),
            dma((ns - 1, 4, heads)),
            dma((lags, 2, heads, ns)),
            dma((lags, 2, heads, ns)),
            dma((lags, 2, heads, ns)),
            dma((lags, 2, heads, ns)),
            dma((ns - 1, 2, heads)),
            dma((ns - 1, 2, heads)),
            dma((ns - 1, 2, heads)),
            dma((ns - 1, 2, heads)),
            dma((2, heads, ns)),
            dma((2, heads, ns)),
            dma((2, heads, ns)),
            dma((2, heads, ns)),
        ],
        compiler_params=pltpu.CompilerParams(
            collective_id=0, has_side_effects=True, vmem_limit_bytes=123 * 2**19
        ),
    )(*flat, conv_weight, block_mask)
    outs = pl.pallas_call(
        hand_on,
        out_shape=[jax.ShapeDtypeStruct((rows, width), BF16)] * 4,
        in_specs=[vmem] * 4,
        out_specs=[pl.BlockSpec(memory_space=pl.ANY)] * 4,
        scratch_shapes=[dma((4,))],
        compiler_params=pltpu.CompilerParams(vmem_limit_bytes=8 * 2**20),
    )(*outs)
    return tuple(x.reshape(query.shape) for x in outs)


def solution(mesh):
    spec = P(("groups", "tm"), "space", None, None)
    return jax.shard_map(
        local,
        mesh=mesh,
        in_specs=(spec, spec, spec, spec, P(), P()),
        out_specs=(spec, spec, spec, spec),
        check_vma=False,
    )
```

```python
import functools
import math

import jax
import jax.numpy as jnp
from jax import lax
from jax.experimental import pallas as pl
from jax.experimental.pallas import tpu as pltpu
from jax.sharding import PartitionSpec as P

HD = 128
MESH = pl.DeviceIdType.MESH
F32 = jnp.float32
BF16 = jnp.bfloat16
NT = (((1,), (1,)), ((), ()))


def kernel(
    n, ns, win, frames, radial,
    q_ref, k_ref, v_ref, d_ref, w_ref, mask_ref,
    o_ref, gq_ref, gk_ref, gv_ref,
    pair, kv, st, ob, gb, gr, ac, ar, rf, rb,
    near, nr, lx, sx_s, sx_r, f_s, f_r, g_s, g_r, ob_s, ob_r, ac_s, ac_r,
    rf_s, rf_r, rb_s, rb_r,
):
    i = lax.axis_index("tm")
    s = lax.axis_index("space")
    rows, width = q_ref.shape
    heads = width // HD // ns
    block = ns * rows
    lags = win - 1
    scale = 1.0 / math.sqrt(HD)
    ins = (q_ref, k_ref, v_ref, d_ref)
    relay = win == 2 and n % 2 == 0
    planes = max(1, n // 2)
    plane = i // 2
    odd = lax.rem(i, 2) == 1
    even = jnp.logical_not(odd)
    via_ahead = heads * (planes - 1 - plane) // planes
    share = max(0, 2 * heads * ns // planes - 1)
    via_back = share * plane
    gate = share * (plane - 1) - jnp.where(plane > 1, 1, 2)

    def cols(slot, h):
        return pl.ds(pl.multiple_of((slot * heads + h) * HD, HD), HD)

    def slab(slot):
        return pl.ds(pl.multiple_of(slot * rows, rows), rows)

    def peer(shift):
        return lax.rem(s + shift, ns)

    def source(shift):
        return lax.rem(s + ns - shift, ns)

    def own_copy(a, h):
        return pltpu.make_async_copy(
            ins[a].at[:, cols(s, h)], pair.at[a, h, slab(s)], lx.at[a, h]
        )

    def pair_copy(shift, a, h):
        return pltpu.make_async_remote_copy(
            src_ref=ins[a].at[:, cols(peer(shift), h)],
            dst_ref=pair.at[a, h, slab(s)],
            send_sem=sx_s.at[shift - 1, a, h],
            recv_sem=sx_r.at[shift - 1, a, h],
            device_id={"space": peer(shift)},
            device_id_type=MESH,
        )

    def ahead_copy(lag, a, h, slot, sem_slot):
        return pltpu.make_async_remote_copy(
            src_ref=near.at[a, :, cols(slot, h)],
            dst_ref=kv.at[lag - 1, a, h, slab(s)],
            send_sem=f_s.at[lag - 1, a, h, slot],
            recv_sem=f_r.at[lag - 1, a, h, sem_slot],
            device_id={"tm": i + lag, "space": slot},
            device_id_type=MESH,
        )

    def back_copy(lag, a, h, slot, sem_slot):
        return pltpu.make_async_remote_copy(
            src_ref=gb.at[lag - 1, a, h, pl.ds(slot * rows, rows)],
            dst_ref=gr.at[lag - 1, a, h, s],
            send_sem=g_s.at[lag - 1, a, h, slot],
            recv_sem=g_r.at[lag - 1, a, h, sem_slot],
            device_id={"tm": i - lag, "space": slot},
            device_id_type=MESH,
        )

    def ahead_first(a, h, slot, sem_slot):
        return pltpu.make_async_remote_copy(
            src_ref=near.at[a, :, cols(slot, h)],
            dst_ref=rf.at[a, h, slab(s)],
            send_sem=f_s.at[0, a, h, slot],
            recv_sem=rf_r.at[a, h, sem_slot],
            device_id={"tm": i - 1, "space": slot},
            device_id_type=MESH,
        )

    def ahead_second(a, h, src):
        return pltpu.make_async_remote_copy(
            src_ref=rf.at[a, h, slab(src)],
            dst_ref=kv.at[0, a, h, slab(src)],
            send_sem=rf_s.at[a, h, src],
            recv_sem=f_r.at[0, a, h, src],
            device_id={"tm": i + 2},
            device_id_type=MESH,
        )

    def back_first(a, h, slot, sem_slot):
        return pltpu.make_async_remote_copy(
            src_ref=gb.at[0, a, h, pl.ds(slot * rows, rows)],
            dst_ref=rb.at[a, h, s],
            send_sem=g_s.at[0, a, h, slot],
            recv_sem=rb_r.at[a, h, sem_slot],
            device_id={"tm": i + 1, "space": slot},
            device_id_type=MESH,
        )

    def back_second(a, h, src):
        return pltpu.make_async_remote_copy(
            src_ref=rb.at[a, h, src],
            dst_ref=gr.at[0, a, h, src],
            send_sem=rb_s.at[a, h, src],
            recv_sem=g_r.at[0, a, h, src],
            device_id={"tm": i - 2},
            device_id_type=MESH,
        )

    def out_copy(shift, b, h):
        return pltpu.make_async_remote_copy(
            src_ref=ob.at[b, h, slab(peer(shift))],
            dst_ref=(o_ref, gq_ref)[b].at[:, cols(s, h)],
            send_sem=ob_s.at[shift - 1, b, h],
            recv_sem=ob_r.at[shift - 1, b, h],
            device_id={"space": peer(shift)},
            device_id_type=MESH,
        )

    def own_grad_copy(shift, a, h):
        return pltpu.make_async_remote_copy(
            src_ref=ac.at[a, h, slab(peer(shift))],
            dst_ref=ar.at[shift - 1, a, h],
            send_sem=ac_s.at[shift - 1, a, h],
            recv_sem=ac_r.at[shift - 1, a, h],
            device_id={"space": peer(shift)},
            device_id_type=MESH,
        )

    barrier = pltpu.get_barrier_semaphore()
    count = ns - 1
    for shift in range(1, ns):
        pl.semaphore_signal(barrier, inc=1, device_id={"space": peer(shift)}, device_id_type=MESH)
    for lag in range(1, win):
        for there, here in ((i + lag, i + lag < n), (i - lag, i >= lag)):
            count = count + ns * jnp.where(here, 1, 0)

            @pl.when(here)
            def _():
                for slot in range(ns):
                    pl.semaphore_signal(
                        barrier, inc=1, device_id={"tm": there, "space": slot}, device_id_type=MESH
                    )

    def fetch_own(h, carry):
        for a in range(4):
            own_copy(a, h).start()
        return carry

    lax.fori_loop(0, heads, fetch_own, 0)
    fetch = [pltpu.make_async_copy(ins[1 + a], near.at[a], nr.at[a]) for a in range(2)]
    for copy in fetch:
        copy.start()
    pl.semaphore_wait(barrier, count)
    for copy in fetch:
        copy.wait()


    def direct(here, far):
        return here if far is None else jnp.logical_and(here, jnp.logical_not(far))

    def send_ahead(h, carry):
        if relay:
            h = lax.rem(h + jnp.where(jnp.logical_and(odd, plane == 0), heads - via_ahead, 0), heads)
        for lag in range(1, win):
            far = jnp.logical_and(odd, h >= heads - via_ahead) if relay else None

            @pl.when(direct(i + lag < n, far))
            def _():
                for a in range(2):
                    for slot in range(ns):
                        ahead_copy(lag, a, h, slot, s).start()

        if relay:

            @pl.when(jnp.logical_and(i + 1 < n, far))
            def _():
                for a in range(2):
                    for slot in range(ns):
                        ahead_first(a, h, slot, s).start()

        return carry

    def send_inputs(h, carry):
        for a in range(4):
            for shift in range(1, ns):
                pair_copy(shift, a, h).start()
        return carry

    lax.fori_loop(0, heads, send_ahead, 0)
    lax.fori_loop(0, heads, send_inputs, 0)

    for lag in range(1, win):

        @pl.when(i < lag)
        def _():
            kv[lag - 1] = jnp.zeros(kv.shape[1:], BF16)

    biases = [None]
    for lag in range(1, win):
        allowed = jnp.logical_and(i >= lag, mask_ref[i, jnp.maximum(i - lag, 0)] > 0)
        biases.append(jnp.where(allowed, 0.0, -jnp.inf).astype(F32))

    chunks = [(lag, c) for lag in range(win) for c in range(ns)]
    span = rows // frames

    def neighbours(a, h):
        low, high = [], []
        for slot in range(ns):
            before, after = (slot + ns - 1) % ns * rows, (slot + 1) % ns * rows
            for f in range(frames):
                at = f * span
                here = slot * rows + at
                low.append(pair[a, h, before + at + span - radial : before + at + span, :])
                low.append(pair[a, h, here : here + span - radial, :])
                high.append(pair[a, h, here + radial : here + span, :])
                high.append(pair[a, h, after + at : after + at + radial, :])
        return (
            jnp.concatenate(low, axis=0).astype(F32),
            jnp.concatenate(high, axis=0).astype(F32),
        )

    def part(a, h, slot):
        return (2 * h + a) * ns + slot

    def send_relayed(h, carry):
        for a in range(2):
            for slot in range(ns):

                @pl.when(jnp.logical_and(jnp.logical_and(even, i >= 1), part(a, h, slot) < via_back))
                def _():
                    back_first(a, h, slot, s).start()

        return carry

    def send_terms(h, carry):
        for lag in range(1, win):
            for a in range(2):
                for slot in range(ns):
                    near = jnp.logical_or(odd, part(a, h, slot) >= via_back) if relay else None

                    @pl.when(i >= lag if near is None else jnp.logical_and(i >= lag, near))
                    def _():
                        back_copy(lag, a, h, slot, s).start()

        return carry

    def own_gate(h, carry):
        for a in range(2):
            for slot in range(ns):

                @pl.when(part(a, h, slot) == gate)
                def _():
                    back_first(a, h, slot, s).wait_send()

        return carry

    def ahead_gate(a, h, slot):
        here = jnp.logical_and(even, jnp.logical_and(i >= 1, gate < 0))
        return jnp.logical_and(here, part(a, h, slot) == 2 * heads * ns + gate)

    def head(h, carry):
        if relay:

            @pl.when(jnp.logical_and(even, jnp.logical_and(gate < 0, h == heads - 1)))
            def _():
                for a in range(2):
                    for slot in range(ns):

                        @pl.when(ahead_gate(a, h, slot))
                        def _():
                            ahead_copy(1, a, h, slot, s).wait_send()

                lax.fori_loop(0, heads - 1, send_terms, 0)


            later = h + 1

            @pl.when(
                jnp.logical_and(
                    jnp.logical_and(even, i + 2 < n),
                    jnp.logical_and(later >= heads - via_ahead, later < heads),
                )
            )
            def _():
                for a in range(2):
                    for src in range(ns):
                        ahead_first(a, later, src, src).wait_recv()
                        ahead_second(a, later, src).start()

        for a in range(4):
            own_copy(a, h).wait()
            for shift in range(1, ns):
                pair_copy(shift, a, h).wait_recv()
        for lag in range(1, win):

            @pl.when(i >= lag)
            def _():
                for a in range(2):
                    for slot in range(ns):
                        ahead_copy(lag, a, h, slot, slot).wait_recv()

        if not relay:

            @pl.when(h == heads - 1)
            def _():
                lax.fori_loop(0, heads - 1, send_terms, 0)

        q = pair[0, h]
        d = pair[3, h]

        def keys(lag, c):
            at = slice(c * rows, (c + 1) * rows)
            return pair[1, h, at, :] if lag == 0 else kv[lag - 1, 0, h, at, :]

        def vals(lag, c):
            at = slice(c * rows, (c + 1) * rows)
            return pair[2, h, at, :] if lag == 0 else kv[lag - 1, 1, h, at, :]

        top = None
        for j, (lag, c) in enumerate(chunks):
            sc = lax.dot_general(keys(lag, c), q, NT, preferred_element_type=F32)
            if lag:
                sc = sc + biases[lag]
            st[j * rows : (j + 1) * rows, :] = sc
            high = jnp.max(sc, axis=0, keepdims=True)
            top = high if top is None else jnp.maximum(top, high)
        total = None
        att = None
        factor = scale * math.log2(math.e)
        for j, (lag, c) in enumerate(chunks):
            p = jnp.exp2((st[j * rows : (j + 1) * rows, :] - top) * factor)
            st[j * rows : (j + 1) * rows, :] = p
            add = jnp.sum(p, axis=0, keepdims=True)
            total = add if total is None else total + add
            term = jnp.dot(vals(lag, c).T, p.astype(BF16), preferred_element_type=F32)
            att = term if att is None else att + term
        inv = 1.0 / total
        att = att * inv
        delta = jnp.sum(d.T.astype(F32) * att, axis=0, keepdims=True)
        v_low, v_high = neighbours(2, h)
        d_low, d_high = neighbours(3, h)
        w0 = w_ref[0:1, cols(s, h)]
        w1 = w_ref[1:2, cols(s, h)]
        w2 = w_ref[2:3, cols(s, h)]
        lepe = w0 * v_low + w1 * pair[2, h].astype(F32) + w2 * v_high
        conv_back = w0 * d_high + w1 * d.astype(F32) + w2 * d_low
        ob[0, h] = (att.T + lepe).astype(BF16)
        gq = None
        for j, (lag, c) in reversed(list(enumerate(chunks))):
            at = slice(c * rows, (c + 1) * rows)
            dp = lax.dot_general(vals(lag, c), d, NT, preferred_element_type=F32)
            p = st[j * rows : (j + 1) * rows, :] * inv
            gv = jnp.dot(p.astype(BF16), d, preferred_element_type=F32)
            ds = (p * (dp - delta)).astype(BF16)
            gk = jnp.dot(ds, q, preferred_element_type=F32) * scale
            term = jnp.dot(keys(lag, c).T, ds, preferred_element_type=F32)
            gq = term if gq is None else gq + term
            if lag:
                gb[lag - 1, 0, h, at, :] = gk.astype(BF16)
                gb[lag - 1, 1, h, at, :] = gv.astype(BF16)
            else:
                ac[0, h, at, :] = gk
                ac[1, h, at, :] = gv + conv_back[at]
        ob[1, h] = (gq * scale).T.astype(BF16)

        if relay:
            send_relayed(h, 0)

        now = h == heads - 1
        if relay:
            now = jnp.logical_or(odd, jnp.logical_and(now, gate < 0))

        @pl.when(now)
        def _():
            send_terms(h, 0)

        for shift in range(1, ns):
            for b in range(2):
                out_copy(shift, b, h).start()
                own_grad_copy(shift, b, h).start()
        o_ref[:, cols(s, h)] = ob[0, h, slab(s), :]
        gq_ref[:, cols(s, h)] = ob[1, h, slab(s), :]
        return carry

    lax.fori_loop(0, heads, head, 0)

    def drain(h, carry):
        for shift in range(1, ns):
            for a in range(4):
                pair_copy(shift, a, h).wait_send()
            for b in range(2):
                out_copy(shift, b, h).wait()
                own_grad_copy(shift, b, h).wait_send()
        for lag in range(1, win):
            for a in range(2):
                for slot in range(ns):

                    left = i + lag < n
                    if relay:
                        left = jnp.logical_and(left, jnp.logical_not(ahead_gate(a, h, slot)))

                    @pl.when(left)
                    def _():
                        ahead_copy(lag, a, h, slot, s).wait_send()

        return carry

    def relay_back(h, carry):
        for a in range(2):

            @pl.when(jnp.logical_and(jnp.logical_and(odd, i >= 2), part(a, h, s) < via_back))
            def _():
                for src in range(ns):
                    back_first(a, h, src, src).wait_recv()
                    back_second(a, h, src).start()

        return carry

    if relay:
        lax.fori_loop(0, heads, relay_back, 0)
    lax.fori_loop(0, heads, drain, 0)
    if relay:

        @pl.when(jnp.logical_and(even, gate >= 0))
        def _():
            lax.fori_loop(0, heads, own_gate, 0)
            lax.fori_loop(0, heads, send_terms, 0)


    def drain_back(h, carry):
        for lag in range(1, win):
            for a in range(2):
                for slot in range(ns):
                    left = i >= lag
                    if relay:
                        passed = jnp.logical_and(even, part(a, h, slot) == gate)
                        left = jnp.logical_and(left, jnp.logical_not(passed))

                    @pl.when(left)
                    def _():
                        back_copy(lag, a, h, slot, s).wait_send()

        return carry

    def drain_relays(h, carry):
        @pl.when(jnp.logical_and(jnp.logical_and(jnp.logical_not(odd), i + 2 < n), h >= heads - via_ahead))
        def _():
            for a in range(2):
                for src in range(ns):
                    ahead_second(a, h, src).wait_send()

        for a in range(2):

            @pl.when(jnp.logical_and(jnp.logical_and(odd, i >= 2), part(a, h, s) < via_back))
            def _():
                for src in range(ns):
                    back_second(a, h, src).wait_send()

        return carry

    def finish(h, carry):
        for shift in range(ns):
            slot = source(shift)
            for a in range(2):
                if shift:
                    own_grad_copy(shift, a, h).wait_recv()
                    base = ar.at[shift - 1, a, h]
                else:
                    base = ac.at[a, h, slab(s)]
                for lag in range(1, win):

                    @pl.when(i + lag < n)
                    def _():
                        pltpu.make_async_remote_copy(
                            src_ref=gb.at[lag - 1, a, h, slab(slot)],
                            dst_ref=gr.at[lag - 1, a, h, slot],
                            send_sem=g_s.at[lag - 1, a, h, slot],
                            recv_sem=g_r.at[lag - 1, a, h, slot],
                            device_id={"space": peer(1)},
                            device_id_type=MESH,
                        ).wait_recv()
                        base[...] = base[...] + gr[lag - 1, a, h, slot].astype(F32)

                (gk_ref, gv_ref)[a][:, cols(slot, h)] = base[...].astype(BF16)
        return carry

    def drain_terms(h, carry):
        drain_back(h, 0)
        if relay:
            drain_relays(h, 0)
        return carry

    lax.fori_loop(0, heads - 1, finish, 0)
    lax.fori_loop(0, heads - 1, drain_terms, 0)
    finish(heads - 1, 0)
    drain_terms(heads - 1, 0)


def hand_on(*refs):
    sems = refs[-1]
    half = len(refs) // 2
    copies = [pltpu.make_async_copy(refs[j], refs[half + j], sems.at[j]) for j in range(half)]
    for copy in copies:
        copy.start()
    for copy in copies:
        copy.wait()


def local(query, key_in, value, upstream, conv_weight, block_mask):
    frames, cells, radial, width = query.shape
    n = lax.axis_size("tm")
    ns = lax.axis_size("space")
    win = max(2, n // 8)
    lags = win - 1
    rows = frames * cells * radial
    heads = width // HD // ns
    block = ns * rows
    flat = [x.reshape(rows, width) for x in (query, key_in, value, upstream)]
    dma = pltpu.SemaphoreType.DMA
    vmem = pl.BlockSpec(memory_space=pltpu.VMEM)
    outs = pl.pallas_call(
        functools.partial(kernel, n, ns, win, frames, radial),
        out_shape=[pltpu.VMEM((rows, width), BF16)] * 4,
        in_specs=[pl.BlockSpec(memory_space=pltpu.HBM)] * 4 + [vmem] + [pl.BlockSpec(memory_space=pltpu.SMEM)],
        out_specs=[vmem] * 4,
        scratch_shapes=[
            pltpu.VMEM((4, heads, block, HD), BF16),
            pltpu.VMEM((lags, 2, heads, block, HD), BF16),
            pltpu.VMEM((win * block, block), F32),
            pltpu.VMEM((2, heads, block, HD), BF16),
            pltpu.VMEM((lags, 2, heads, block, HD), BF16),
            pltpu.VMEM((lags, 2, heads, ns, rows, HD), BF16),
            pltpu.VMEM((2, heads, block, HD), F32),
            pltpu.VMEM((ns - 1, 2, heads, rows, HD), F32),
            pltpu.VMEM((2, heads, block, HD), BF16),
            pltpu.VMEM((2, heads, ns, rows, HD), BF16),
            pltpu.VMEM((2, rows, width), BF16),
            dma((2,)),
            dma((4, heads)),
            dma((ns - 1, 4, heads)),
            dma((ns - 1, 4, heads)),
            dma((lags, 2, heads, ns)),
            dma((lags, 2, heads, ns)),
            dma((lags, 2, heads, ns)),
            dma((lags, 2, heads, ns)),
            dma((ns - 1, 2, heads)),
            dma((ns - 1, 2, heads)),
            dma((ns - 1, 2, heads)),
            dma((ns - 1, 2, heads)),
            dma((2, heads, ns)),
            dma((2, heads, ns)),
            dma((2, heads, ns)),
            dma((2, heads, ns)),
        ],
        compiler_params=pltpu.CompilerParams(
            collective_id=0, has_side_effects=True, vmem_limit_bytes=123 * 2**19
        ),
    )(*flat, conv_weight, block_mask)
    outs = pl.pallas_call(
        hand_on,
        out_shape=[jax.ShapeDtypeStruct((rows, width), BF16)] * 4,
        in_specs=[vmem] * 4,
        out_specs=[pl.BlockSpec(memory_space=pl.ANY)] * 4,
        scratch_shapes=[dma((4,))],
        compiler_params=pltpu.CompilerParams(vmem_limit_bytes=8 * 2**20),
    )(*outs)
    return tuple(x.reshape(query.shape) for x in outs)


def solution(mesh):
    spec = P(("groups", "tm"), "space", None, None)
    return jax.shard_map(
        local,
        mesh=mesh,
        in_specs=(spec, spec, spec, spec, P(), P()),
        out_specs=(spec, spec, spec, spec),
        check_vma=False,
    )
```

```python
import functools
import math

import jax
import jax.numpy as jnp
from jax import lax
from jax.experimental import pallas as pl
from jax.experimental.pallas import tpu as pltpu
from jax.sharding import PartitionSpec as P

HD = 128
MESH = pl.DeviceIdType.MESH
F32 = jnp.float32
BF16 = jnp.bfloat16
NT = (((1,), (1,)), ((), ()))


def kernel(
    n, ns, win, frames, radial,
    q_ref, k_ref, v_ref, d_ref, taps_ref, blocks_ref,
    o_ref, gq_ref, gk_ref, gv_ref,
    pair, kv, st, ob, gb, gr, ac, ar, rf, rb,
    w_ref, mask_ref, near, nr, lx, sx_s, sx_r, f_s, f_r, g_s, g_r, ob_s, ob_r, ac_s, ac_r,
    rf_s, rf_r, rb_s, rb_r,
):
    i = lax.axis_index("tm")
    s = lax.axis_index("space")
    rows, width = q_ref.shape
    heads = width // HD // ns
    block = ns * rows
    lags = win - 1
    scale = 1.0 / math.sqrt(HD)
    ins = (q_ref, k_ref, v_ref, d_ref)
    relay = win == 2 and n % 2 == 0
    planes = max(1, n // 2)
    plane = i // 2
    odd = lax.rem(i, 2) == 1
    even = jnp.logical_not(odd)
    via_ahead = heads * (planes - 1 - plane) // planes
    share = max(0, 2 * heads * ns // planes - 1)
    via_back = share * plane
    gate = share * (plane - 1) - jnp.where(plane > 1, 1, 2)

    def cols(slot, h):
        return pl.ds(pl.multiple_of((slot * heads + h) * HD, HD), HD)

    def slab(slot):
        return pl.ds(pl.multiple_of(slot * rows, rows), rows)

    def peer(shift):
        return lax.rem(s + shift, ns)

    def source(shift):
        return lax.rem(s + ns - shift, ns)

    def own_copy(a, h):
        return pltpu.make_async_copy(
            ins[a].at[:, cols(s, h)], pair.at[a, h, slab(s)], lx.at[a, h]
        )

    def pair_copy(shift, a, h):
        return pltpu.make_async_remote_copy(
            src_ref=ins[a].at[:, cols(peer(shift), h)],
            dst_ref=pair.at[a, h, slab(s)],
            send_sem=sx_s.at[shift - 1, a, h],
            recv_sem=sx_r.at[shift - 1, a, h],
            device_id={"space": peer(shift)},
            device_id_type=MESH,
        )

    def ahead_copy(lag, a, h, slot, sem_slot):
        return pltpu.make_async_remote_copy(
            src_ref=near.at[a, :, cols(slot, h)],
            dst_ref=kv.at[lag - 1, a, h, slab(s)],
            send_sem=f_s.at[lag - 1, a, h, slot],
            recv_sem=f_r.at[lag - 1, a, h, sem_slot],
            device_id={"tm": i + lag, "space": slot},
            device_id_type=MESH,
        )

    def back_copy(lag, a, h, slot, sem_slot):
        return pltpu.make_async_remote_copy(
            src_ref=gb.at[lag - 1, a, h, pl.ds(slot * rows, rows)],
            dst_ref=gr.at[lag - 1, a, h, s],
            send_sem=g_s.at[lag - 1, a, h, slot],
            recv_sem=g_r.at[lag - 1, a, h, sem_slot],
            device_id={"tm": i - lag, "space": slot},
            device_id_type=MESH,
        )

    def ahead_first(a, h, slot, sem_slot):
        return pltpu.make_async_remote_copy(
            src_ref=near.at[a, :, cols(slot, h)],
            dst_ref=rf.at[a, h, slab(s)],
            send_sem=f_s.at[0, a, h, slot],
            recv_sem=rf_r.at[a, h, sem_slot],
            device_id={"tm": i - 1, "space": slot},
            device_id_type=MESH,
        )

    def ahead_second(a, h, src):
        return pltpu.make_async_remote_copy(
            src_ref=rf.at[a, h, slab(src)],
            dst_ref=kv.at[0, a, h, slab(src)],
            send_sem=rf_s.at[a, h, src],
            recv_sem=f_r.at[0, a, h, src],
            device_id={"tm": i + 2},
            device_id_type=MESH,
        )

    def back_first(a, h, slot, sem_slot):
        return pltpu.make_async_remote_copy(
            src_ref=gb.at[0, a, h, pl.ds(slot * rows, rows)],
            dst_ref=rb.at[a, h, s],
            send_sem=g_s.at[0, a, h, slot],
            recv_sem=rb_r.at[a, h, sem_slot],
            device_id={"tm": i + 1, "space": slot},
            device_id_type=MESH,
        )

    def back_second(a, h, src):
        return pltpu.make_async_remote_copy(
            src_ref=rb.at[a, h, src],
            dst_ref=gr.at[0, a, h, src],
            send_sem=rb_s.at[a, h, src],
            recv_sem=g_r.at[0, a, h, src],
            device_id={"tm": i - 2},
            device_id_type=MESH,
        )

    def out_copy(shift, b, h):
        return pltpu.make_async_remote_copy(
            src_ref=ob.at[b, h, slab(peer(shift))],
            dst_ref=(o_ref, gq_ref)[b].at[:, cols(s, h)],
            send_sem=ob_s.at[shift - 1, b, h],
            recv_sem=ob_r.at[shift - 1, b, h],
            device_id={"space": peer(shift)},
            device_id_type=MESH,
        )

    def own_grad_copy(shift, a, h):
        return pltpu.make_async_remote_copy(
            src_ref=ac.at[a, h, slab(peer(shift))],
            dst_ref=ar.at[shift - 1, a, h],
            send_sem=ac_s.at[shift - 1, a, h],
            recv_sem=ac_r.at[shift - 1, a, h],
            device_id={"space": peer(shift)},
            device_id_type=MESH,
        )

    barrier = pltpu.get_barrier_semaphore()
    count = ns - 1
    for shift in range(1, ns):
        pl.semaphore_signal(barrier, inc=1, device_id={"space": peer(shift)}, device_id_type=MESH)
    for lag in range(1, win):
        for there, here in ((i + lag, i + lag < n), (i - lag, i >= lag)):
            count = count + ns * jnp.where(here, 1, 0)

            @pl.when(here)
            def _():
                for slot in range(ns):
                    pl.semaphore_signal(
                        barrier, inc=1, device_id={"tm": there, "space": slot}, device_id_type=MESH
                    )

    def fetch_own(h, carry):
        for a in range(4):
            own_copy(a, h).start()
        return carry

    lax.fori_loop(0, heads, fetch_own, 0)
    fetch = [pltpu.make_async_copy(ins[1 + a], near.at[a], nr.at[a]) for a in range(2)]
    fetch_small = [
        pltpu.make_async_copy(taps_ref, w_ref, nr.at[2]),
        pltpu.make_async_copy(blocks_ref, mask_ref, nr.at[3]),
    ]
    for copy in fetch_small:
        copy.start()
    for copy in fetch:
        copy.start()
    pl.semaphore_wait(barrier, count)
    for copy in fetch:
        copy.wait()


    def direct(here, far):
        return here if far is None else jnp.logical_and(here, jnp.logical_not(far))

    def send_ahead(h, carry):
        if relay:
            h = lax.rem(h + jnp.where(jnp.logical_and(odd, plane == 0), heads - via_ahead, 0), heads)
        for lag in range(1, win):
            far = jnp.logical_and(odd, h >= heads - via_ahead) if relay else None

            @pl.when(direct(i + lag < n, far))
            def _():
                for a in range(2):
                    for slot in range(ns):
                        ahead_copy(lag, a, h, slot, s).start()

        if relay:

            @pl.when(jnp.logical_and(i + 1 < n, far))
            def _():
                for a in range(2):
                    for slot in range(ns):
                        ahead_first(a, h, slot, s).start()

        return carry

    def send_inputs(h, carry):
        for a in range(4):
            for shift in range(1, ns):
                pair_copy(shift, a, h).start()
        return carry

    lax.fori_loop(0, heads, send_ahead, 0)
    lax.fori_loop(0, heads, send_inputs, 0)

    for lag in range(1, win):

        @pl.when(i < lag)
        def _():
            kv[lag - 1] = jnp.zeros(kv.shape[1:], BF16)

    for copy in fetch_small:
        copy.wait()
    biases = [None]
    for lag in range(1, win):
        allowed = jnp.logical_and(i >= lag, mask_ref[i, jnp.maximum(i - lag, 0)] > 0)
        biases.append(jnp.where(allowed, 0.0, -jnp.inf).astype(F32))

    chunks = [(lag, c) for lag in range(win) for c in range(ns)]
    span = rows // frames

    def neighbours(a, h):
        low, high = [], []
        for slot in range(ns):
            before, after = (slot + ns - 1) % ns * rows, (slot + 1) % ns * rows
            for f in range(frames):
                at = f * span
                here = slot * rows + at
                low.append(pair[a, h, before + at + span - radial : before + at + span, :])
                low.append(pair[a, h, here : here + span - radial, :])
                high.append(pair[a, h, here + radial : here + span, :])
                high.append(pair[a, h, after + at : after + at + radial, :])
        return (
            jnp.concatenate(low, axis=0).astype(F32),
            jnp.concatenate(high, axis=0).astype(F32),
        )

    def part(a, h, slot):
        return (2 * h + a) * ns + slot

    def send_relayed(h, carry):
        for a in range(2):
            for slot in range(ns):

                @pl.when(jnp.logical_and(jnp.logical_and(even, i >= 1), part(a, h, slot) < via_back))
                def _():
                    back_first(a, h, slot, s).start()

        return carry

    def send_terms(h, carry):
        for lag in range(1, win):
            for a in range(2):
                for slot in range(ns):
                    near = jnp.logical_or(odd, part(a, h, slot) >= via_back) if relay else None

                    @pl.when(i >= lag if near is None else jnp.logical_and(i >= lag, near))
                    def _():
                        back_copy(lag, a, h, slot, s).start()

        return carry

    def own_gate(h, carry):
        for a in range(2):
            for slot in range(ns):

                @pl.when(part(a, h, slot) == gate)
                def _():
                    back_first(a, h, slot, s).wait_send()

        return carry

    def ahead_gate(a, h, slot):
        here = jnp.logical_and(even, jnp.logical_and(i >= 1, gate < 0))
        return jnp.logical_and(here, part(a, h, slot) == 2 * heads * ns + gate)

    def head(h, carry):
        if relay:

            @pl.when(jnp.logical_and(even, jnp.logical_and(gate < 0, h == heads - 1)))
            def _():
                for a in range(2):
                    for slot in range(ns):

                        @pl.when(ahead_gate(a, h, slot))
                        def _():
                            ahead_copy(1, a, h, slot, s).wait_send()

                lax.fori_loop(0, heads - 1, send_terms, 0)


            later = h + 1

            @pl.when(
                jnp.logical_and(
                    jnp.logical_and(even, i + 2 < n),
                    jnp.logical_and(later >= heads - via_ahead, later < heads),
                )
            )
            def _():
                for a in range(2):
                    for src in range(ns):
                        ahead_first(a, later, src, src).wait_recv()
                        ahead_second(a, later, src).start()

        for a in range(4):
            own_copy(a, h).wait()
            for shift in range(1, ns):
                pair_copy(shift, a, h).wait_recv()
        for lag in range(1, win):

            @pl.when(i >= lag)
            def _():
                for a in range(2):
                    for slot in range(ns):
                        ahead_copy(lag, a, h, slot, slot).wait_recv()

        if not relay:

            @pl.when(h == heads - 1)
            def _():
                lax.fori_loop(0, heads - 1, send_terms, 0)

        q = pair[0, h]
        d = pair[3, h]

        def keys(lag, c):
            at = slice(c * rows, (c + 1) * rows)
            return pair[1, h, at, :] if lag == 0 else kv[lag - 1, 0, h, at, :]

        def vals(lag, c):
            at = slice(c * rows, (c + 1) * rows)
            return pair[2, h, at, :] if lag == 0 else kv[lag - 1, 1, h, at, :]

        top = None
        for j, (lag, c) in enumerate(chunks):
            sc = lax.dot_general(keys(lag, c), q, NT, preferred_element_type=F32)
            if lag:
                sc = sc + biases[lag]
            st[j * rows : (j + 1) * rows, :] = sc
            high = jnp.max(sc, axis=0, keepdims=True)
            top = high if top is None else jnp.maximum(top, high)
        total = None
        att = None
        factor = scale * math.log2(math.e)
        for j, (lag, c) in enumerate(chunks):
            p = jnp.exp2((st[j * rows : (j + 1) * rows, :] - top) * factor)
            st[j * rows : (j + 1) * rows, :] = p
            add = jnp.sum(p, axis=0, keepdims=True)
            total = add if total is None else total + add
            term = jnp.dot(vals(lag, c).T, p.astype(BF16), preferred_element_type=F32)
            att = term if att is None else att + term
        inv = 1.0 / total
        att = att * inv
        delta = jnp.sum(d.T.astype(F32) * att, axis=0, keepdims=True)
        v_low, v_high = neighbours(2, h)
        d_low, d_high = neighbours(3, h)
        w0 = w_ref[0:1, cols(s, h)]
        w1 = w_ref[1:2, cols(s, h)]
        w2 = w_ref[2:3, cols(s, h)]
        lepe = w0 * v_low + w1 * pair[2, h].astype(F32) + w2 * v_high
        conv_back = w0 * d_high + w1 * d.astype(F32) + w2 * d_low
        ob[0, h] = (att.T + lepe).astype(BF16)
        gq = None
        for j, (lag, c) in reversed(list(enumerate(chunks))):
            at = slice(c * rows, (c + 1) * rows)
            dp = lax.dot_general(vals(lag, c), d, NT, preferred_element_type=F32)
            p = st[j * rows : (j + 1) * rows, :] * inv
            gv = jnp.dot(p.astype(BF16), d, preferred_element_type=F32)
            ds = (p * (dp - delta)).astype(BF16)
            gk = jnp.dot(ds, q, preferred_element_type=F32) * scale
            term = jnp.dot(keys(lag, c).T, ds, preferred_element_type=F32)
            gq = term if gq is None else gq + term
            if lag:
                gb[lag - 1, 0, h, at, :] = gk.astype(BF16)
                gb[lag - 1, 1, h, at, :] = gv.astype(BF16)
            else:
                ac[0, h, at, :] = gk
                ac[1, h, at, :] = gv + conv_back[at]
        ob[1, h] = (gq * scale).T.astype(BF16)

        if relay:
            send_relayed(h, 0)

        now = h == heads - 1
        if relay:
            now = jnp.logical_or(odd, jnp.logical_and(now, gate < 0))

        @pl.when(now)
        def _():
            send_terms(h, 0)

        for shift in range(1, ns):
            for b in range(2):
                out_copy(shift, b, h).start()
                own_grad_copy(shift, b, h).start()
        o_ref[:, cols(s, h)] = ob[0, h, slab(s), :]
        gq_ref[:, cols(s, h)] = ob[1, h, slab(s), :]
        return carry

    lax.fori_loop(0, heads, head, 0)

    def drain(h, carry):
        for shift in range(1, ns):
            for a in range(4):
                pair_copy(shift, a, h).wait_send()
            for b in range(2):
                out_copy(shift, b, h).wait()
                own_grad_copy(shift, b, h).wait_send()
        for lag in range(1, win):
            for a in range(2):
                for slot in range(ns):

                    left = i + lag < n
                    if relay:
                        left = jnp.logical_and(left, jnp.logical_not(ahead_gate(a, h, slot)))

                    @pl.when(left)
                    def _():
                        ahead_copy(lag, a, h, slot, s).wait_send()

        return carry

    def relay_back(h, carry):
        for a in range(2):

            @pl.when(jnp.logical_and(jnp.logical_and(odd, i >= 2), part(a, h, s) < via_back))
            def _():
                for src in range(ns):
                    back_first(a, h, src, src).wait_recv()
                    back_second(a, h, src).start()

        return carry

    if relay:
        lax.fori_loop(0, heads, relay_back, 0)
    lax.fori_loop(0, heads, drain, 0)
    if relay:

        @pl.when(jnp.logical_and(even, gate >= 0))
        def _():
            lax.fori_loop(0, heads, own_gate, 0)
            lax.fori_loop(0, heads, send_terms, 0)


    def drain_back(h, carry):
        for lag in range(1, win):
            for a in range(2):
                for slot in range(ns):
                    left = i >= lag
                    if relay:
                        passed = jnp.logical_and(even, part(a, h, slot) == gate)
                        left = jnp.logical_and(left, jnp.logical_not(passed))

                    @pl.when(left)
                    def _():
                        back_copy(lag, a, h, slot, s).wait_send()

        return carry

    def drain_relays(h, carry):
        @pl.when(jnp.logical_and(jnp.logical_and(jnp.logical_not(odd), i + 2 < n), h >= heads - via_ahead))
        def _():
            for a in range(2):
                for src in range(ns):
                    ahead_second(a, h, src).wait_send()

        for a in range(2):

            @pl.when(jnp.logical_and(jnp.logical_and(odd, i >= 2), part(a, h, s) < via_back))
            def _():
                for src in range(ns):
                    back_second(a, h, src).wait_send()

        return carry

    def finish(h, carry):
        for shift in range(ns):
            slot = source(shift)
            for a in range(2):
                if shift:
                    own_grad_copy(shift, a, h).wait_recv()
                    base = ar.at[shift - 1, a, h]
                else:
                    base = ac.at[a, h, slab(s)]
                for lag in range(1, win):

                    @pl.when(i + lag < n)
                    def _():
                        pltpu.make_async_remote_copy(
                            src_ref=gb.at[lag - 1, a, h, slab(slot)],
                            dst_ref=gr.at[lag - 1, a, h, slot],
                            send_sem=g_s.at[lag - 1, a, h, slot],
                            recv_sem=g_r.at[lag - 1, a, h, slot],
                            device_id={"space": peer(1)},
                            device_id_type=MESH,
                        ).wait_recv()
                        base[...] = base[...] + gr[lag - 1, a, h, slot].astype(F32)

                (gk_ref, gv_ref)[a][:, cols(slot, h)] = base[...].astype(BF16)
        return carry

    def drain_terms(h, carry):
        drain_back(h, 0)
        if relay:
            drain_relays(h, 0)
        return carry

    lax.fori_loop(0, heads - 1, finish, 0)
    lax.fori_loop(0, heads - 1, drain_terms, 0)
    finish(heads - 1, 0)
    drain_terms(heads - 1, 0)


def hand_on(*refs):
    sems = refs[-1]
    half = len(refs) // 2
    copies = [pltpu.make_async_copy(refs[j], refs[half + j], sems.at[j]) for j in range(half)]
    for copy in copies:
        copy.start()
    for copy in copies:
        copy.wait()


def local(query, key_in, value, upstream, conv_weight, block_mask):
    frames, cells, radial, width = query.shape
    n = lax.axis_size("tm")
    ns = lax.axis_size("space")
    win = max(2, n // 8)
    lags = win - 1
    rows = frames * cells * radial
    heads = width // HD // ns
    block = ns * rows
    flat = [x.reshape(rows, width) for x in (query, key_in, value, upstream)]
    dma = pltpu.SemaphoreType.DMA
    vmem = pl.BlockSpec(memory_space=pltpu.VMEM)
    outs = pl.pallas_call(
        functools.partial(kernel, n, ns, win, frames, radial),
        out_shape=[pltpu.VMEM((rows, width), BF16)] * 4,
        in_specs=[pl.BlockSpec(memory_space=pltpu.HBM)] * 6,
        out_specs=[vmem] * 4,
        scratch_shapes=[
            pltpu.VMEM((4, heads, block, HD), BF16),
            pltpu.VMEM((lags, 2, heads, block, HD), BF16),
            pltpu.VMEM((win * block, block), F32),
            pltpu.VMEM((2, heads, block, HD), BF16),
            pltpu.VMEM((lags, 2, heads, block, HD), BF16),
            pltpu.VMEM((lags, 2, heads, ns, rows, HD), BF16),
            pltpu.VMEM((2, heads, block, HD), F32),
            pltpu.VMEM((ns - 1, 2, heads, rows, HD), F32),
            pltpu.VMEM((2, heads, block, HD), BF16),
            pltpu.VMEM((2, heads, ns, rows, HD), BF16),
            pltpu.VMEM(conv_weight.shape, F32),
            pltpu.SMEM(block_mask.shape, jnp.int32),
            pltpu.VMEM((2, rows, width), BF16),
            dma((4,)),
            dma((4, heads)),
            dma((ns - 1, 4, heads)),
            dma((ns - 1, 4, heads)),
            dma((lags, 2, heads, ns)),
            dma((lags, 2, heads, ns)),
            dma((lags, 2, heads, ns)),
            dma((lags, 2, heads, ns)),
            dma((ns - 1, 2, heads)),
            dma((ns - 1, 2, heads)),
            dma((ns - 1, 2, heads)),
            dma((ns - 1, 2, heads)),
            dma((2, heads, ns)),
            dma((2, heads, ns)),
            dma((2, heads, ns)),
            dma((2, heads, ns)),
        ],
        compiler_params=pltpu.CompilerParams(
            collective_id=0, has_side_effects=True, vmem_limit_bytes=123 * 2**19
        ),
    )(*flat, conv_weight, block_mask)
    outs = pl.pallas_call(
        hand_on,
        out_shape=[jax.ShapeDtypeStruct((rows, width), BF16)] * 4,
        in_specs=[vmem] * 4,
        out_specs=[pl.BlockSpec(memory_space=pl.ANY)] * 4,
        scratch_shapes=[dma((4,))],
        compiler_params=pltpu.CompilerParams(vmem_limit_bytes=8 * 2**20),
    )(*outs)
    return tuple(x.reshape(query.shape) for x in outs)


def solution(mesh):
    spec = P(("groups", "tm"), "space", None, None)
    return jax.shard_map(
        local,
        mesh=mesh,
        in_specs=(spec, spec, spec, spec, P(), P()),
        out_specs=(spec, spec, spec, spec),
        check_vma=False,
    )
```

```python
import functools
import math

import jax
import jax.numpy as jnp
from jax import lax
from jax.experimental import pallas as pl
from jax.experimental.pallas import tpu as pltpu
from jax.sharding import PartitionSpec as P

HD = 128
MESH = pl.DeviceIdType.MESH
F32 = jnp.float32
BF16 = jnp.bfloat16
NT = (((1,), (1,)), ((), ()))


def kernel(
    n, ns, win, frames, radial,
    q_ref, k_ref, v_ref, d_ref, taps_ref, blocks_ref,
    o_ref, gq_ref, gk_ref, gv_ref,
    pair, kv, st, ob, gb, gr, ac, ar, rf, rb,
    w_ref, mask_ref, near, nr, lx, sx_s, sx_r, f_s, f_r, g_s, g_r, ob_s, ob_r, ac_s, ac_r,
    rf_s, rf_r, rb_s, rb_r,
):
    i = lax.axis_index("tm")
    s = lax.axis_index("space")
    rows, width = q_ref.shape
    heads = width // HD // ns
    block = ns * rows
    lags = win - 1
    scale = 1.0 / math.sqrt(HD)
    ins = (q_ref, k_ref, v_ref, d_ref)
    relay = win == 2 and n % 2 == 0
    planes = max(1, n // 2)
    plane = i // 2
    odd = lax.rem(i, 2) == 1
    even = jnp.logical_not(odd)
    via_ahead = heads * (planes - 1 - plane) // planes
    share = max(0, 2 * heads * ns // planes - 1)

    def relayed_of(plane, core):
        return jnp.where(plane > 0, share * plane + jnp.where(core == 0, 1, 0), 0)

    via_back = relayed_of(plane, s)
    gate = relayed_of(plane - 1, s) - 1

    def cols(slot, h):
        return pl.ds(pl.multiple_of((slot * heads + h) * HD, HD), HD)

    def slab(slot):
        return pl.ds(pl.multiple_of(slot * rows, rows), rows)

    def peer(shift):
        return lax.rem(s + shift, ns)

    def source(shift):
        return lax.rem(s + ns - shift, ns)

    def own_copy(a, h):
        return pltpu.make_async_copy(
            ins[a].at[:, cols(s, h)], pair.at[a, h, slab(s)], lx.at[a, h]
        )

    def pair_copy(shift, a, h):
        return pltpu.make_async_remote_copy(
            src_ref=ins[a].at[:, cols(peer(shift), h)],
            dst_ref=pair.at[a, h, slab(s)],
            send_sem=sx_s.at[shift - 1, a, h],
            recv_sem=sx_r.at[shift - 1, a, h],
            device_id={"space": peer(shift)},
            device_id_type=MESH,
        )

    def ahead_copy(lag, a, h, slot, sem_slot):
        return pltpu.make_async_remote_copy(
            src_ref=near.at[a, :, cols(slot, h)],
            dst_ref=kv.at[lag - 1, a, h, slab(s)],
            send_sem=f_s.at[lag - 1, a, h, slot],
            recv_sem=f_r.at[lag - 1, a, h, sem_slot],
            device_id={"tm": i + lag, "space": slot},
            device_id_type=MESH,
        )

    def back_copy(lag, a, h, slot, sem_slot):
        return pltpu.make_async_remote_copy(
            src_ref=gb.at[lag - 1, a, h, pl.ds(slot * rows, rows)],
            dst_ref=gr.at[lag - 1, a, h, s],
            send_sem=g_s.at[lag - 1, a, h, slot],
            recv_sem=g_r.at[lag - 1, a, h, sem_slot],
            device_id={"tm": i - lag, "space": slot},
            device_id_type=MESH,
        )

    def ahead_first(a, h, slot, sem_slot):
        return pltpu.make_async_remote_copy(
            src_ref=near.at[a, :, cols(slot, h)],
            dst_ref=rf.at[a, h, slab(s)],
            send_sem=f_s.at[0, a, h, slot],
            recv_sem=rf_r.at[a, h, sem_slot],
            device_id={"tm": i - 1, "space": slot},
            device_id_type=MESH,
        )

    def ahead_second(a, h, src):
        return pltpu.make_async_remote_copy(
            src_ref=rf.at[a, h, slab(src)],
            dst_ref=kv.at[0, a, h, slab(src)],
            send_sem=rf_s.at[a, h, src],
            recv_sem=f_r.at[0, a, h, src],
            device_id={"tm": i + 2},
            device_id_type=MESH,
        )

    def back_first(a, h, slot, sem_slot):
        return pltpu.make_async_remote_copy(
            src_ref=gb.at[0, a, h, pl.ds(slot * rows, rows)],
            dst_ref=rb.at[a, h, s],
            send_sem=g_s.at[0, a, h, slot],
            recv_sem=rb_r.at[a, h, sem_slot],
            device_id={"tm": i + 1, "space": slot},
            device_id_type=MESH,
        )

    def back_second(a, h, src):
        return pltpu.make_async_remote_copy(
            src_ref=rb.at[a, h, src],
            dst_ref=gr.at[0, a, h, src],
            send_sem=rb_s.at[a, h, src],
            recv_sem=g_r.at[0, a, h, src],
            device_id={"tm": i - 2},
            device_id_type=MESH,
        )

    def out_copy(shift, b, h):
        return pltpu.make_async_remote_copy(
            src_ref=ob.at[b, h, slab(peer(shift))],
            dst_ref=(o_ref, gq_ref)[b].at[:, cols(s, h)],
            send_sem=ob_s.at[shift - 1, b, h],
            recv_sem=ob_r.at[shift - 1, b, h],
            device_id={"space": peer(shift)},
            device_id_type=MESH,
        )

    def own_grad_copy(shift, a, h):
        return pltpu.make_async_remote_copy(
            src_ref=ac.at[a, h, slab(peer(shift))],
            dst_ref=ar.at[shift - 1, a, h],
            send_sem=ac_s.at[shift - 1, a, h],
            recv_sem=ac_r.at[shift - 1, a, h],
            device_id={"space": peer(shift)},
            device_id_type=MESH,
        )

    barrier = pltpu.get_barrier_semaphore()
    count = ns - 1
    for shift in range(1, ns):
        pl.semaphore_signal(barrier, inc=1, device_id={"space": peer(shift)}, device_id_type=MESH)
    for lag in range(1, win):
        for there, here in ((i + lag, i + lag < n), (i - lag, i >= lag)):
            count = count + ns * jnp.where(here, 1, 0)

            @pl.when(here)
            def _():
                for slot in range(ns):
                    pl.semaphore_signal(
                        barrier, inc=1, device_id={"tm": there, "space": slot}, device_id_type=MESH
                    )

    fetch = [pltpu.make_async_copy(ins[1 + a], near.at[a], nr.at[a]) for a in range(2)]
    for copy in fetch:
        copy.start()
    fetch_small = [
        pltpu.make_async_copy(taps_ref, w_ref, nr.at[2]),
        pltpu.make_async_copy(blocks_ref, mask_ref, nr.at[3]),
    ]
    for copy in fetch_small:
        copy.start()
    def fetch_own(h, carry):
        for a in range(4):
            own_copy(a, h).start()
        return carry

    lax.fori_loop(0, heads, fetch_own, 0)
    pl.semaphore_wait(barrier, count)
    for copy in fetch:
        copy.wait()


    def direct(here, far):
        return here if far is None else jnp.logical_and(here, jnp.logical_not(far))

    def send_ahead(h, carry):
        if relay:
            h = lax.rem(h + jnp.where(jnp.logical_and(odd, plane == 0), heads - via_ahead, 0), heads)
        for lag in range(1, win):
            far = jnp.logical_and(odd, h >= heads - via_ahead) if relay else None

            @pl.when(direct(i + lag < n, far))
            def _():
                for a in range(2):
                    for slot in range(ns):
                        ahead_copy(lag, a, h, slot, s).start()

        if relay:

            @pl.when(jnp.logical_and(i + 1 < n, far))
            def _():
                for a in range(2):
                    for slot in range(ns):
                        ahead_first(a, h, slot, s).start()

        return carry

    def send_inputs(h, carry):
        for a in range(4):
            for shift in range(1, ns):
                pair_copy(shift, a, h).start()
        return carry

    lax.fori_loop(0, heads, send_ahead, 0)
    lax.fori_loop(0, heads, send_inputs, 0)

    for lag in range(1, win):

        @pl.when(i < lag)
        def _():
            kv[lag - 1] = jnp.zeros(kv.shape[1:], BF16)

    for copy in fetch_small:
        copy.wait()
    biases = [None]
    for lag in range(1, win):
        allowed = jnp.logical_and(i >= lag, mask_ref[i, jnp.maximum(i - lag, 0)] > 0)
        biases.append(jnp.where(allowed, 0.0, -jnp.inf).astype(F32))

    chunks = [(lag, c) for lag in range(win) for c in range(ns)]
    span = rows // frames

    def neighbours(a, h):
        low, high = [], []
        for slot in range(ns):
            before, after = (slot + ns - 1) % ns * rows, (slot + 1) % ns * rows
            for f in range(frames):
                at = f * span
                here = slot * rows + at
                low.append(pair[a, h, before + at + span - radial : before + at + span, :])
                low.append(pair[a, h, here : here + span - radial, :])
                high.append(pair[a, h, here + radial : here + span, :])
                high.append(pair[a, h, after + at : after + at + radial, :])
        return (
            jnp.concatenate(low, axis=0).astype(F32),
            jnp.concatenate(high, axis=0).astype(F32),
        )

    def part(a, h, slot):
        return (2 * h + a) * ns + slot

    def send_relayed(h, carry):
        for a in range(2):
            for slot in range(ns):

                @pl.when(jnp.logical_and(jnp.logical_and(even, i >= 1), part(a, h, slot) < via_back))
                def _():
                    back_first(a, h, slot, s).start()

        return carry

    def send_terms(h, carry):
        for lag in range(1, win):
            for a in range(2):
                for slot in range(ns):
                    near = jnp.logical_or(odd, part(a, h, slot) >= via_back) if relay else None

                    @pl.when(i >= lag if near is None else jnp.logical_and(i >= lag, near))
                    def _():
                        back_copy(lag, a, h, slot, s).start()

        return carry

    def own_gate(h, carry):
        for a in range(2):
            for slot in range(ns):

                @pl.when(part(a, h, slot) == gate)
                def _():
                    back_first(a, h, slot, s).wait_send()

        return carry

    def ahead_gate(a, h, slot):
        here = jnp.logical_and(even, jnp.logical_and(i >= 1, gate < 0))
        return jnp.logical_and(here, part(a, h, slot) == 2 * heads * ns + gate)

    def head(h, carry):
        if relay:

            @pl.when(jnp.logical_and(even, jnp.logical_and(gate < 0, h == heads - 1)))
            def _():
                for a in range(2):
                    for slot in range(ns):

                        @pl.when(ahead_gate(a, h, slot))
                        def _():
                            ahead_copy(1, a, h, slot, s).wait_send()

                lax.fori_loop(0, heads - 1, send_terms, 0)


            later = h + 1

            @pl.when(
                jnp.logical_and(
                    jnp.logical_and(even, i + 2 < n),
                    jnp.logical_and(later >= heads - via_ahead, later < heads),
                )
            )
            def _():
                for a in range(2):
                    for src in range(ns):
                        ahead_first(a, later, src, src).wait_recv()
                        ahead_second(a, later, src).start()

        for a in range(4):
            own_copy(a, h).wait()
            for shift in range(1, ns):
                pair_copy(shift, a, h).wait_recv()
        for lag in range(1, win):

            @pl.when(i >= lag)
            def _():
                for a in range(2):
                    for slot in range(ns):
                        ahead_copy(lag, a, h, slot, slot).wait_recv()

        if not relay:

            @pl.when(h == heads - 1)
            def _():
                lax.fori_loop(0, heads - 1, send_terms, 0)

        q = pair[0, h]
        d = pair[3, h]

        def keys(lag, c):
            at = slice(c * rows, (c + 1) * rows)
            return pair[1, h, at, :] if lag == 0 else kv[lag - 1, 0, h, at, :]

        def vals(lag, c):
            at = slice(c * rows, (c + 1) * rows)
            return pair[2, h, at, :] if lag == 0 else kv[lag - 1, 1, h, at, :]

        top = None
        for j, (lag, c) in enumerate(chunks):
            sc = lax.dot_general(keys(lag, c), q, NT, preferred_element_type=F32)
            if lag:
                sc = sc + biases[lag]
            st[j * rows : (j + 1) * rows, :] = sc
            high = jnp.max(sc, axis=0, keepdims=True)
            top = high if top is None else jnp.maximum(top, high)
        total = None
        att = None
        factor = scale * math.log2(math.e)
        for j, (lag, c) in enumerate(chunks):
            p = jnp.exp2((st[j * rows : (j + 1) * rows, :] - top) * factor)
            st[j * rows : (j + 1) * rows, :] = p
            add = jnp.sum(p, axis=0, keepdims=True)
            total = add if total is None else total + add
            term = jnp.dot(vals(lag, c).T, p.astype(BF16), preferred_element_type=F32)
            att = term if att is None else att + term
        inv = 1.0 / total
        att = att * inv
        delta = jnp.sum(d.T.astype(F32) * att, axis=0, keepdims=True)
        v_low, v_high = neighbours(2, h)
        d_low, d_high = neighbours(3, h)
        w0 = w_ref[0:1, cols(s, h)]
        w1 = w_ref[1:2, cols(s, h)]
        w2 = w_ref[2:3, cols(s, h)]
        lepe = w0 * v_low + w1 * pair[2, h].astype(F32) + w2 * v_high
        conv_back = w0 * d_high + w1 * d.astype(F32) + w2 * d_low
        ob[0, h] = (att.T + lepe).astype(BF16)
        gq = None
        for j, (lag, c) in reversed(list(enumerate(chunks))):
            at = slice(c * rows, (c + 1) * rows)
            dp = lax.dot_general(vals(lag, c), d, NT, preferred_element_type=F32)
            p = st[j * rows : (j + 1) * rows, :] * inv
            gv = jnp.dot(p.astype(BF16), d, preferred_element_type=F32)
            ds = (p * (dp - delta)).astype(BF16)
            gk = jnp.dot(ds, q, preferred_element_type=F32) * scale
            term = jnp.dot(keys(lag, c).T, ds, preferred_element_type=F32)
            gq = term if gq is None else gq + term
            if lag:
                gb[lag - 1, 0, h, at, :] = gk.astype(BF16)
                gb[lag - 1, 1, h, at, :] = gv.astype(BF16)
            else:
                ac[0, h, at, :] = gk
                ac[1, h, at, :] = gv + conv_back[at]
        ob[1, h] = (gq * scale).T.astype(BF16)

        if relay:
            send_relayed(h, 0)

        now = h == heads - 1
        if relay:
            now = jnp.logical_or(odd, jnp.logical_and(now, gate < 0))

        @pl.when(now)
        def _():
            send_terms(h, 0)

        for shift in range(1, ns):
            for b in range(2):
                out_copy(shift, b, h).start()
                own_grad_copy(shift, b, h).start()
        o_ref[:, cols(s, h)] = ob[0, h, slab(s), :]
        gq_ref[:, cols(s, h)] = ob[1, h, slab(s), :]
        return carry

    lax.fori_loop(0, heads, head, 0)

    def drain(h, carry):
        for shift in range(1, ns):
            for a in range(4):
                pair_copy(shift, a, h).wait_send()
            for b in range(2):
                out_copy(shift, b, h).wait()
                own_grad_copy(shift, b, h).wait_send()
        for lag in range(1, win):
            for a in range(2):
                for slot in range(ns):
                    left = i + lag < n
                    if relay:
                        left = jnp.logical_and(left, jnp.logical_not(ahead_gate(a, h, slot)))

                    @pl.when(left)
                    def _():
                        ahead_copy(lag, a, h, slot, s).wait_send()

        return carry

    def relay_back(h, carry):
        for a in range(2):
            for src in range(ns):

                @pl.when(jnp.logical_and(jnp.logical_and(odd, i >= 2), part(a, h, s) < relayed_of(plane, src)))
                def _():
                    back_first(a, h, src, src).wait_recv()
                    back_second(a, h, src).start()

        return carry

    if relay:
        lax.fori_loop(0, heads, relay_back, 0)
    lax.fori_loop(0, heads, drain, 0)
    if relay:

        @pl.when(jnp.logical_and(even, gate >= 0))
        def _():
            lax.fori_loop(0, heads, own_gate, 0)
            lax.fori_loop(0, heads, send_terms, 0)


    def drain_back(h, carry):
        for lag in range(1, win):
            for a in range(2):
                for slot in range(ns):
                    left = i >= lag
                    if relay:
                        passed = jnp.logical_and(even, part(a, h, slot) == gate)
                        left = jnp.logical_and(left, jnp.logical_not(passed))

                    @pl.when(left)
                    def _():
                        back_copy(lag, a, h, slot, s).wait_send()

        return carry

    def drain_relays(h, carry):
        @pl.when(jnp.logical_and(jnp.logical_and(jnp.logical_not(odd), i + 2 < n), h >= heads - via_ahead))
        def _():
            for a in range(2):
                for src in range(ns):
                    ahead_second(a, h, src).wait_send()

        for a in range(2):

            for src in range(ns):

                @pl.when(jnp.logical_and(jnp.logical_and(odd, i >= 2), part(a, h, s) < relayed_of(plane, src)))
                def _():
                    back_second(a, h, src).wait_send()

        return carry

    def term_arrival(lag, a, h, slot):
        return pltpu.make_async_remote_copy(
            src_ref=gb.at[lag - 1, a, h, slab(slot)],
            dst_ref=gr.at[lag - 1, a, h, slot],
            send_sem=g_s.at[lag - 1, a, h, slot],
            recv_sem=g_r.at[lag - 1, a, h, slot],
            device_id={"space": peer(1)},
            device_id_type=MESH,
        )

    def finish(h, carry):
        for shift in range(1, ns):
            for a in range(2):
                own_grad_copy(shift, a, h).wait_recv()
        def settle(lags_here):
            for a in range(2):
                for shift in range(ns):
                    slot = source(shift)
                    total = (ar.at[shift - 1, a, h] if shift else ac.at[a, h, slab(s)])[...]
                    for lag in range(1, lags_here + 1):
                        term_arrival(lag, a, h, slot).wait_recv()
                        total = total + gr[lag - 1, a, h, slot].astype(F32)
                    (gk_ref, gv_ref)[a][:, cols(slot, h)] = total.astype(BF16)

        for here in range(win):

            @pl.when(i + here == n - 1 if here < lags else i + here < n)
            def _():
                settle(here)

        return carry

    def drain_terms(h, carry):
        drain_back(h, 0)
        if relay:
            drain_relays(h, 0)
        return carry

    lax.fori_loop(0, heads - 1, finish, 0)
    lax.fori_loop(0, heads, drain_terms, 0)
    finish(heads - 1, 0)


def hand_on(*refs):
    sems = refs[-1]
    half = len(refs) // 2
    copies = [pltpu.make_async_copy(refs[j], refs[half + j], sems.at[j]) for j in range(half)]
    for copy in copies:
        copy.start()
    for copy in copies:
        copy.wait()


def local(query, key_in, value, upstream, conv_weight, block_mask):
    frames, cells, radial, width = query.shape
    n = lax.axis_size("tm")
    ns = lax.axis_size("space")
    win = max(2, n // 8)
    lags = win - 1
    rows = frames * cells * radial
    heads = width // HD // ns
    block = ns * rows
    flat = [x.reshape(rows, width) for x in (query, key_in, value, upstream)]
    dma = pltpu.SemaphoreType.DMA
    vmem = pl.BlockSpec(memory_space=pltpu.VMEM)
    outs = pl.pallas_call(
        functools.partial(kernel, n, ns, win, frames, radial),
        out_shape=[pltpu.VMEM((rows, width), BF16)] * 4,
        in_specs=[pl.BlockSpec(memory_space=pltpu.HBM)] * 6,
        out_specs=[vmem] * 4,
        scratch_shapes=[
            pltpu.VMEM((4, heads, block, HD), BF16),
            pltpu.VMEM((lags, 2, heads, block, HD), BF16),
            pltpu.VMEM((win * block, block), F32),
            pltpu.VMEM((2, heads, block, HD), BF16),
            pltpu.VMEM((lags, 2, heads, block, HD), BF16),
            pltpu.VMEM((lags, 2, heads, ns, rows, HD), BF16),
            pltpu.VMEM((2, heads, block, HD), F32),
            pltpu.VMEM((ns - 1, 2, heads, rows, HD), F32),
            pltpu.VMEM((2, heads, block, HD), BF16),
            pltpu.VMEM((2, heads, ns, rows, HD), BF16),
            pltpu.VMEM(conv_weight.shape, F32),
            pltpu.SMEM(block_mask.shape, jnp.int32),
            pltpu.VMEM((2, rows, width), BF16),
            dma((4,)),
            dma((4, heads)),
            dma((ns - 1, 4, heads)),
            dma((ns - 1, 4, heads)),
            dma((lags, 2, heads, ns)),
            dma((lags, 2, heads, ns)),
            dma((lags, 2, heads, ns)),
            dma((lags, 2, heads, ns)),
            dma((ns - 1, 2, heads)),
            dma((ns - 1, 2, heads)),
            dma((ns - 1, 2, heads)),
            dma((ns - 1, 2, heads)),
            dma((2, heads, ns)),
            dma((2, heads, ns)),
            dma((2, heads, ns)),
            dma((2, heads, ns)),
        ],
        compiler_params=pltpu.CompilerParams(
            collective_id=0, has_side_effects=True, vmem_limit_bytes=123 * 2**19
        ),
    )(*flat, conv_weight, block_mask)
    outs = pl.pallas_call(
        hand_on,
        out_shape=[jax.ShapeDtypeStruct((rows, width), BF16)] * 4,
        in_specs=[vmem] * 4,
        out_specs=[pl.BlockSpec(memory_space=pl.ANY)] * 4,
        scratch_shapes=[dma((4,))],
        compiler_params=pltpu.CompilerParams(vmem_limit_bytes=8 * 2**20),
    )(*outs)
    return tuple(x.reshape(query.shape) for x in outs)


def solution(mesh):
    spec = P(("groups", "tm"), "space", None, None)
    return jax.shard_map(
        local,
        mesh=mesh,
        in_specs=(spec, spec, spec, spec, P(), P()),
        out_specs=(spec, spec, spec, spec),
        check_vma=False,
    )
```

```python
import functools
import math

import jax
import jax.numpy as jnp
from jax import lax
from jax.experimental import pallas as pl
from jax.experimental.pallas import tpu as pltpu
from jax.sharding import PartitionSpec as P

HD = 128
MESH = pl.DeviceIdType.MESH
F32 = jnp.float32
BF16 = jnp.bfloat16
NT = (((1,), (1,)), ((), ()))


def kernel(
    n, ns, win, frames, radial,
    q_ref, k_ref, v_ref, d_ref, taps_ref, blocks_ref,
    o_ref, gq_ref, gk_ref, gv_ref,
    pair, kv, st, ob, gb, gr, ac, ar, rf, rb,
    w_ref, mask_ref, near, nr, lx, sx_s, sx_r, f_s, f_r, g_s, g_r, ob_s, ob_r, ac_s, ac_r,
    rf_s, rf_r, rb_s, rb_r,
):
    i = lax.axis_index("tm")
    s = lax.axis_index("space")
    rows, width = q_ref.shape
    heads = width // HD // ns
    block = ns * rows
    lags = win - 1
    scale = 1.0 / math.sqrt(HD)
    ins = (q_ref, k_ref, v_ref, d_ref)
    relay = win == 2 and n % 2 == 0
    planes = max(1, n // 2)
    plane = i // 2
    odd = lax.rem(i, 2) == 1
    even = jnp.logical_not(odd)
    via_ahead = heads * (planes - 1 - plane) // planes
    share = max(0, 2 * heads * ns // planes - 1)

    def relayed_of(plane, core):
        return jnp.where(plane > 0, share * plane + jnp.where(core == 0, 1, 0), 0)

    via_back = relayed_of(plane, s)
    gate = relayed_of(plane - 1, s) - 1

    def cols(slot, h):
        return pl.ds(pl.multiple_of((slot * heads + h) * HD, HD), HD)

    def slab(slot):
        return pl.ds(pl.multiple_of(slot * rows, rows), rows)

    def peer(shift):
        return lax.rem(s + shift, ns)

    def source(shift):
        return lax.rem(s + ns - shift, ns)

    def own_copy(a, h):
        return pltpu.make_async_copy(
            ins[a].at[:, cols(s, h)], pair.at[a, h, slab(s)], lx.at[a, h]
        )

    def pair_copy(shift, a, h):
        return pltpu.make_async_remote_copy(
            src_ref=ins[a].at[:, cols(peer(shift), h)],
            dst_ref=pair.at[a, h, slab(s)],
            send_sem=sx_s.at[shift - 1, a, h],
            recv_sem=sx_r.at[shift - 1, a, h],
            device_id={"space": peer(shift)},
            device_id_type=MESH,
        )

    def ahead_copy(lag, a, h, slot, sem_slot):
        return pltpu.make_async_remote_copy(
            src_ref=near.at[a, :, cols(slot, h)],
            dst_ref=kv.at[lag - 1, a, h, slab(s)],
            send_sem=f_s.at[lag - 1, a, h, slot],
            recv_sem=f_r.at[lag - 1, a, h, sem_slot],
            device_id={"tm": lax.rem(i + lag, n), "space": slot},
            device_id_type=MESH,
        )

    def back_copy(lag, a, h, slot, sem_slot):
        return pltpu.make_async_remote_copy(
            src_ref=gb.at[lag - 1, a, h, pl.ds(slot * rows, rows)],
            dst_ref=gr.at[lag - 1, a, h, s],
            send_sem=g_s.at[lag - 1, a, h, slot],
            recv_sem=g_r.at[lag - 1, a, h, sem_slot],
            device_id={"tm": i - lag, "space": slot},
            device_id_type=MESH,
        )

    def ahead_first(a, h, slot, sem_slot):
        return pltpu.make_async_remote_copy(
            src_ref=near.at[a, :, cols(slot, h)],
            dst_ref=rf.at[a, h, slab(s)],
            send_sem=f_s.at[0, a, h, slot],
            recv_sem=rf_r.at[a, h, sem_slot],
            device_id={"tm": lax.rem(i + n - 1, n), "space": slot},
            device_id_type=MESH,
        )

    def ahead_second(a, h, src):
        return pltpu.make_async_remote_copy(
            src_ref=rf.at[a, h, slab(src)],
            dst_ref=kv.at[0, a, h, slab(src)],
            send_sem=rf_s.at[a, h, src],
            recv_sem=f_r.at[0, a, h, src],
            device_id={"tm": i + 2},
            device_id_type=MESH,
        )

    def back_first(a, h, slot, sem_slot):
        return pltpu.make_async_remote_copy(
            src_ref=gb.at[0, a, h, pl.ds(slot * rows, rows)],
            dst_ref=rb.at[a, h, s],
            send_sem=g_s.at[0, a, h, slot],
            recv_sem=rb_r.at[a, h, sem_slot],
            device_id={"tm": lax.rem(i + 1, n), "space": slot},
            device_id_type=MESH,
        )

    def back_second(a, h, src):
        return pltpu.make_async_remote_copy(
            src_ref=rb.at[a, h, src],
            dst_ref=gr.at[0, a, h, src],
            send_sem=rb_s.at[a, h, src],
            recv_sem=g_r.at[0, a, h, src],
            device_id={"tm": i - 2},
            device_id_type=MESH,
        )

    def out_copy(shift, b, h):
        return pltpu.make_async_remote_copy(
            src_ref=ob.at[b, h, slab(peer(shift))],
            dst_ref=(o_ref, gq_ref)[b].at[:, cols(s, h)],
            send_sem=ob_s.at[shift - 1, b, h],
            recv_sem=ob_r.at[shift - 1, b, h],
            device_id={"space": peer(shift)},
            device_id_type=MESH,
        )

    def own_grad_copy(shift, a, h):
        return pltpu.make_async_remote_copy(
            src_ref=ac.at[a, h, slab(peer(shift))],
            dst_ref=ar.at[shift - 1, a, h],
            send_sem=ac_s.at[shift - 1, a, h],
            recv_sem=ac_r.at[shift - 1, a, h],
            device_id={"space": peer(shift)},
            device_id_type=MESH,
        )

    barrier = pltpu.get_barrier_semaphore()
    count = ns - 1
    for shift in range(1, ns):
        pl.semaphore_signal(barrier, inc=1, device_id={"space": peer(shift)}, device_id_type=MESH)
    for lag in range(1, win):
        for there, here in ((i + lag, i + lag < n), (i - lag, i >= lag)):
            count = count + ns * jnp.where(here, 1, 0)

            @pl.when(here)
            def _():
                for slot in range(ns):
                    pl.semaphore_signal(
                        barrier, inc=1, device_id={"tm": there, "space": slot}, device_id_type=MESH
                    )

    fetch = [pltpu.make_async_copy(ins[1 + a], near.at[a], nr.at[a]) for a in range(2)]
    for copy in fetch:
        copy.start()
    fetch_small = [
        pltpu.make_async_copy(taps_ref, w_ref, nr.at[2]),
        pltpu.make_async_copy(blocks_ref, mask_ref, nr.at[3]),
    ]
    for copy in fetch_small:
        copy.start()
    def fetch_own(h, carry):
        for a in range(4):
            own_copy(a, h).start()
        return carry

    lax.fori_loop(0, heads, fetch_own, 0)
    pl.semaphore_wait(barrier, count)
    for copy in fetch:
        copy.wait()


    def direct(here, far):
        return here if far is None else jnp.logical_and(here, jnp.logical_not(far))

    def send_ahead(h, carry):
        if relay:
            h = lax.rem(h + jnp.where(jnp.logical_and(odd, plane == 0), heads - via_ahead, 0), heads)
        for lag in range(1, win):
            far = jnp.logical_and(odd, h >= heads - via_ahead) if relay else None

            @pl.when(direct(i + lag < n, far))
            def _():
                for a in range(2):
                    for slot in range(ns):
                        ahead_copy(lag, a, h, slot, s).start()

        if relay:

            @pl.when(jnp.logical_and(i + 1 < n, far))
            def _():
                for a in range(2):
                    for slot in range(ns):
                        ahead_first(a, h, slot, s).start()

        return carry

    def send_inputs(h, carry):
        for a in range(4):
            for shift in range(1, ns):
                pair_copy(shift, a, h).start()
        return carry

    lax.fori_loop(0, heads, send_ahead, 0)
    lax.fori_loop(0, heads, send_inputs, 0)

    for lag in range(1, win):

        @pl.when(i < lag)
        def _():
            kv[lag - 1] = jnp.zeros(kv.shape[1:], BF16)

    for copy in fetch_small:
        copy.wait()
    biases = [None]
    for lag in range(1, win):
        allowed = jnp.logical_and(i >= lag, mask_ref[i, jnp.maximum(i - lag, 0)] > 0)
        biases.append(jnp.where(allowed, 0.0, -jnp.inf).astype(F32))

    chunks = [(lag, c) for lag in range(win) for c in range(ns)]
    span = rows // frames

    def neighbours(a, h):
        low, high = [], []
        for slot in range(ns):
            before, after = (slot + ns - 1) % ns * rows, (slot + 1) % ns * rows
            for f in range(frames):
                at = f * span
                here = slot * rows + at
                low.append(pair[a, h, before + at + span - radial : before + at + span, :])
                low.append(pair[a, h, here : here + span - radial, :])
                high.append(pair[a, h, here + radial : here + span, :])
                high.append(pair[a, h, after + at : after + at + radial, :])
        return (
            jnp.concatenate(low, axis=0).astype(F32),
            jnp.concatenate(high, axis=0).astype(F32),
        )

    def part(a, h, slot):
        return (2 * h + a) * ns + slot

    def send_relayed(h, carry):
        for a in range(2):
            for slot in range(ns):

                @pl.when(jnp.logical_and(jnp.logical_and(even, i >= 1), part(a, h, slot) < via_back))
                def _():
                    back_first(a, h, slot, s).start()

        return carry

    def send_terms(h, carry):
        for lag in range(1, win):
            for a in range(2):
                for slot in range(ns):
                    near = jnp.logical_or(odd, part(a, h, slot) >= via_back) if relay else None

                    @pl.when(i >= lag if near is None else jnp.logical_and(i >= lag, near))
                    def _():
                        back_copy(lag, a, h, slot, s).start()

        return carry

    def own_gate(h, carry):
        for a in range(2):
            for slot in range(ns):

                @pl.when(part(a, h, slot) == gate)
                def _():
                    back_first(a, h, slot, s).wait_send()

        return carry

    def ahead_gate(a, h, slot):
        here = jnp.logical_and(even, jnp.logical_and(i >= 1, gate < 0))
        return jnp.logical_and(here, part(a, h, slot) == 2 * heads * ns + gate)

    def head(h, carry):
        if relay:

            @pl.when(jnp.logical_and(even, jnp.logical_and(gate < 0, h == heads - 1)))
            def _():
                for a in range(2):
                    for slot in range(ns):

                        @pl.when(ahead_gate(a, h, slot))
                        def _():
                            ahead_copy(1, a, h, slot, s).wait_send()

                lax.fori_loop(0, heads - 1, send_terms, 0)


            later = h + 1

            @pl.when(
                jnp.logical_and(
                    jnp.logical_and(even, i + 2 < n),
                    jnp.logical_and(later >= heads - via_ahead, later < heads),
                )
            )
            def _():
                for a in range(2):
                    for src in range(ns):
                        ahead_first(a, later, src, src).wait_recv()
                        ahead_second(a, later, src).start()

        for a in range(4):
            own_copy(a, h).wait()
            for shift in range(1, ns):
                pair_copy(shift, a, h).wait_recv()
        for lag in range(1, win):

            @pl.when(i >= lag)
            def _():
                for a in range(2):
                    for slot in range(ns):
                        ahead_copy(lag, a, h, slot, slot).wait_recv()

        if not relay:

            @pl.when(h == heads - 1)
            def _():
                lax.fori_loop(0, heads - 1, send_terms, 0)

        q = pair[0, h]
        d = pair[3, h]

        def keys(lag, c):
            at = slice(c * rows, (c + 1) * rows)
            return pair[1, h, at, :] if lag == 0 else kv[lag - 1, 0, h, at, :]

        def vals(lag, c):
            at = slice(c * rows, (c + 1) * rows)
            return pair[2, h, at, :] if lag == 0 else kv[lag - 1, 1, h, at, :]

        top = None
        for j, (lag, c) in enumerate(chunks):
            sc = lax.dot_general(keys(lag, c), q, NT, preferred_element_type=F32)
            if lag:
                sc = sc + biases[lag]
            st[j * rows : (j + 1) * rows, :] = sc
            high = jnp.max(sc, axis=0, keepdims=True)
            top = high if top is None else jnp.maximum(top, high)
        total = None
        att = None
        factor = scale * math.log2(math.e)
        for j, (lag, c) in enumerate(chunks):
            p = jnp.exp2((st[j * rows : (j + 1) * rows, :] - top) * factor)
            st[j * rows : (j + 1) * rows, :] = p
            add = jnp.sum(p, axis=0, keepdims=True)
            total = add if total is None else total + add
            term = jnp.dot(vals(lag, c).T, p.astype(BF16), preferred_element_type=F32)
            att = term if att is None else att + term
        inv = 1.0 / total
        att = att * inv
        delta = jnp.sum(d.T.astype(F32) * att, axis=0, keepdims=True)
        v_low, v_high = neighbours(2, h)
        d_low, d_high = neighbours(3, h)
        w0 = w_ref[0:1, cols(s, h)]
        w1 = w_ref[1:2, cols(s, h)]
        w2 = w_ref[2:3, cols(s, h)]
        lepe = w0 * v_low + w1 * pair[2, h].astype(F32) + w2 * v_high
        conv_back = w0 * d_high + w1 * d.astype(F32) + w2 * d_low
        ob[0, h] = (att.T + lepe).astype(BF16)
        gq = None
        for j, (lag, c) in reversed(list(enumerate(chunks))):
            at = slice(c * rows, (c + 1) * rows)
            dp = lax.dot_general(vals(lag, c), d, NT, preferred_element_type=F32)
            p = st[j * rows : (j + 1) * rows, :] * inv
            gv = jnp.dot(p.astype(BF16), d, preferred_element_type=F32)
            ds = (p * (dp - delta)).astype(BF16)
            gk = jnp.dot(ds, q, preferred_element_type=F32) * scale
            term = jnp.dot(keys(lag, c).T, ds, preferred_element_type=F32)
            gq = term if gq is None else gq + term
            if lag:
                gb[lag - 1, 0, h, at, :] = gk.astype(BF16)
                gb[lag - 1, 1, h, at, :] = gv.astype(BF16)
            else:
                ac[0, h, at, :] = gk
                ac[1, h, at, :] = gv + conv_back[at]
        ob[1, h] = (gq * scale).T.astype(BF16)

        if relay:
            send_relayed(h, 0)

        now = h == heads - 1
        if relay:
            now = jnp.logical_or(odd, jnp.logical_and(now, gate < 0))

        @pl.when(now)
        def _():
            send_terms(h, 0)

        for shift in range(1, ns):
            for b in range(2):
                out_copy(shift, b, h).start()
                own_grad_copy(shift, b, h).start()
        o_ref[:, cols(s, h)] = ob[0, h, slab(s), :]
        gq_ref[:, cols(s, h)] = ob[1, h, slab(s), :]
        return carry

    lax.fori_loop(0, heads, head, 0)

    def drain(h, carry):
        for shift in range(1, ns):
            for a in range(4):
                pair_copy(shift, a, h).wait_send()
            for b in range(2):
                out_copy(shift, b, h).wait()
                own_grad_copy(shift, b, h).wait_send()
        for lag in range(1, win):
            for a in range(2):
                for slot in range(ns):
                    left = i + lag < n
                    if relay:
                        left = jnp.logical_and(left, jnp.logical_not(ahead_gate(a, h, slot)))

                    @pl.when(left)
                    def _():
                        ahead_copy(lag, a, h, slot, s).wait_send()

        return carry

    def relay_back(h, carry):
        for a in range(2):
            for src in range(ns):

                @pl.when(jnp.logical_and(jnp.logical_and(odd, i >= 2), part(a, h, s) < relayed_of(plane, src)))
                def _():
                    back_first(a, h, src, src).wait_recv()
                    back_second(a, h, src).start()

        return carry

    if relay:
        lax.fori_loop(0, heads, relay_back, 0)
    lax.fori_loop(0, heads, drain, 0)
    if relay:

        @pl.when(jnp.logical_and(even, gate >= 0))
        def _():
            lax.fori_loop(0, heads, own_gate, 0)
            lax.fori_loop(0, heads, send_terms, 0)


    def drain_back(h, carry):
        for lag in range(1, win):
            for a in range(2):
                for slot in range(ns):
                    left = i >= lag
                    if relay:
                        passed = jnp.logical_and(even, part(a, h, slot) == gate)
                        left = jnp.logical_and(left, jnp.logical_not(passed))

                    @pl.when(left)
                    def _():
                        back_copy(lag, a, h, slot, s).wait_send()

        return carry

    def drain_relays(h, carry):
        @pl.when(jnp.logical_and(jnp.logical_and(jnp.logical_not(odd), i + 2 < n), h >= heads - via_ahead))
        def _():
            for a in range(2):
                for src in range(ns):
                    ahead_second(a, h, src).wait_send()

        for a in range(2):

            for src in range(ns):

                @pl.when(jnp.logical_and(jnp.logical_and(odd, i >= 2), part(a, h, s) < relayed_of(plane, src)))
                def _():
                    back_second(a, h, src).wait_send()

        return carry

    def term_arrival(lag, a, h, slot):
        return pltpu.make_async_remote_copy(
            src_ref=gb.at[lag - 1, a, h, slab(slot)],
            dst_ref=gr.at[lag - 1, a, h, slot],
            send_sem=g_s.at[lag - 1, a, h, slot],
            recv_sem=g_r.at[lag - 1, a, h, slot],
            device_id={"space": peer(1)},
            device_id_type=MESH,
        )

    def finish(h, carry):
        for shift in range(1, ns):
            for a in range(2):
                own_grad_copy(shift, a, h).wait_recv()
        def settle(lags_here):
            for a in range(2):
                for shift in range(ns):
                    slot = source(shift)
                    total = (ar.at[shift - 1, a, h] if shift else ac.at[a, h, slab(s)])[...]
                    for lag in range(1, lags_here + 1):
                        term_arrival(lag, a, h, slot).wait_recv()
                        total = total + gr[lag - 1, a, h, slot].astype(F32)
                    (gk_ref, gv_ref)[a][:, cols(slot, h)] = total.astype(BF16)

        for here in range(win):

            @pl.when(i + here == n - 1 if here < lags else i + here < n)
            def _():
                settle(here)

        return carry

    def drain_terms(h, carry):
        drain_back(h, 0)
        if relay:
            drain_relays(h, 0)
        return carry

    lax.fori_loop(0, heads - 1, finish, 0)
    lax.fori_loop(0, heads, drain_terms, 0)
    finish(heads - 1, 0)


def hand_on(*refs):
    sems = refs[-1]
    half = len(refs) // 2
    copies = [pltpu.make_async_copy(refs[j], refs[half + j], sems.at[j]) for j in range(half)]
    for copy in copies:
        copy.start()
    for copy in copies:
        copy.wait()


def local(query, key_in, value, upstream, conv_weight, block_mask):
    frames, cells, radial, width = query.shape
    n = lax.axis_size("tm")
    ns = lax.axis_size("space")
    win = max(2, n // 8)
    lags = win - 1
    rows = frames * cells * radial
    heads = width // HD // ns
    block = ns * rows
    flat = [x.reshape(rows, width) for x in (query, key_in, value, upstream)]
    dma = pltpu.SemaphoreType.DMA
    vmem = pl.BlockSpec(memory_space=pltpu.VMEM)
    outs = pl.pallas_call(
        functools.partial(kernel, n, ns, win, frames, radial),
        out_shape=[pltpu.VMEM((rows, width), BF16)] * 4,
        in_specs=[pl.BlockSpec(memory_space=pltpu.HBM)] * 6,
        out_specs=[vmem] * 4,
        scratch_shapes=[
            pltpu.VMEM((4, heads, block, HD), BF16),
            pltpu.VMEM((lags, 2, heads, block, HD), BF16),
            pltpu.VMEM((win * block, block), F32),
            pltpu.VMEM((2, heads, block, HD), BF16),
            pltpu.VMEM((lags, 2, heads, block, HD), BF16),
            pltpu.VMEM((lags, 2, heads, ns, rows, HD), BF16),
            pltpu.VMEM((2, heads, block, HD), F32),
            pltpu.VMEM((ns - 1, 2, heads, rows, HD), F32),
            pltpu.VMEM((2, heads, block, HD), BF16),
            pltpu.VMEM((2, heads, ns, rows, HD), BF16),
            pltpu.VMEM(conv_weight.shape, F32),
            pltpu.SMEM(block_mask.shape, jnp.int32),
            pltpu.VMEM((2, rows, width), BF16),
            dma((4,)),
            dma((4, heads)),
            dma((ns - 1, 4, heads)),
            dma((ns - 1, 4, heads)),
            dma((lags, 2, heads, ns)),
            dma((lags, 2, heads, ns)),
            dma((lags, 2, heads, ns)),
            dma((lags, 2, heads, ns)),
            dma((ns - 1, 2, heads)),
            dma((ns - 1, 2, heads)),
            dma((ns - 1, 2, heads)),
            dma((ns - 1, 2, heads)),
            dma((2, heads, ns)),
            dma((2, heads, ns)),
            dma((2, heads, ns)),
            dma((2, heads, ns)),
        ],
        compiler_params=pltpu.CompilerParams(
            collective_id=0, has_side_effects=True, vmem_limit_bytes=123 * 2**19
        ),
    )(*flat, conv_weight, block_mask)
    outs = pl.pallas_call(
        hand_on,
        out_shape=[jax.ShapeDtypeStruct((rows, width), BF16)] * 4,
        in_specs=[vmem] * 4,
        out_specs=[pl.BlockSpec(memory_space=pl.ANY)] * 4,
        scratch_shapes=[dma((4,))],
        compiler_params=pltpu.CompilerParams(vmem_limit_bytes=8 * 2**20),
    )(*outs)
    return tuple(x.reshape(query.shape) for x in outs)


def solution(mesh):
    spec = P(("groups", "tm"), "space", None, None)
    return jax.shard_map(
        local,
        mesh=mesh,
        in_specs=(spec, spec, spec, spec, P(), P()),
        out_specs=(spec, spec, spec, spec),
        check_vma=False,
    )
```
